32 devices in a mesh: seq: 16 (over z, x, core), head: 2 (over y).
Axes of the slice: x: 2, y: 2, z: 4, core: 2. Of those that a mesh axis runs over, the one named last changes fastest.
Arguments:
- queries: bfloat16 [8192, 3072], P(('seq', 'head'))
- keys: bfloat16 [8192, 3072], P(('seq', 'head'))
- values: bfloat16 [8192, 3072], P(('seq', 'head')), may hold values from -6 to 6
- kv_blocks: int32 [64, 64], replicated, may hold values from 0 to 63, as said below
- block_counts: int32 [64, 16], replicated, may hold values from 0 to 4, as said below
Outputs:
- attended: bfloat16 [8192, 3072], P(('seq', 'head'))
The draws below stay inside these ranges and needn't reach their ends.
Inputs may be any that keep to these rules, and one draw needn't show every extreme that they name: `kv_blocks`: slot f * 4 + j names a key block of frame f, as a global block index f * 4 + local; the valid slots of one query block and frame name distinct blocks; slots at or beyond block_counts carry a block of the same frame and no meaning. With e the distance between frame f and the frame of query block b: block_counts[b, f] is 4 where e is 0, at most 2 where e is 1, at most 1 where e is 2, 3 or a power of two, and 0 otherwise; each of these largest values is taken by the first query block of every frame.
All inputs are finite; a program needn't handle non-finite values.
Results may differ from the reference program's by a relative error of at most 0.02.
Values may be sent and summed in bfloat16 or wider, within the bound.
A program may use at most 128 MiB of HBM per device.

```python
import jax
import jax.numpy as jnp
from jax import lax

HEADS = 24
HD = 128
FTOK = 512
BLK = 128
SLOTS = 4
D = 3072
FRAMES = 16
TOKENS = 8192
QBLOCKS = 64


def block_tables(key):
    frame_blocks = FTOK // BLK
    block_ids = jnp.arange(QBLOCKS, dtype=jnp.int32)
    owner_frame = block_ids // frame_blocks
    block_place = block_ids % frame_blocks
    others = jnp.arange(FRAMES, dtype=jnp.int32)
    distance = jnp.abs(owner_frame[:, None] - others[None, :])
    power_two = (distance >= 4) & (distance & distance - 1 == 0)
    limits = jnp.where(distance == 0, SLOTS, jnp.where(distance == 1, 2, jnp.where((distance <= 3) | power_two, 1, 0))).astype(jnp.int32)
    random_counts = jax.random.randint(jax.random.fold_in(key, 13), (QBLOCKS, FRAMES), 0, 3, dtype=jnp.int32)
    counts = jnp.where(distance == 0, SLOTS, jnp.where(block_place[:, None] == 0, limits, jnp.minimum(limits, random_counts))).astype(jnp.int32)
    widths = jnp.maximum(limits, 1)
    jitter = jax.random.randint(jax.random.fold_in(key, 12), (QBLOCKS, FRAMES), 0, SLOTS, dtype=jnp.int32)
    first_block = jnp.clip(block_place[:, None] - jitter % widths, 0, frame_blocks - widths)
    slot_ids = jnp.arange(SLOTS, dtype=jnp.int32)
    offsets = jnp.where(slot_ids[None, None, :] < counts[:, :, None], slot_ids[None, None, :], 0)
    local_ids = first_block[:, :, None] + offsets
    block_lists = (others[None, :, None] * frame_blocks + local_ids).reshape(QBLOCKS, FRAMES * SLOTS)
    return (block_lists.astype(jnp.int32), counts)


def key_field(key):
    array_shape = (FRAMES * FTOK, HEADS * HD)
    return jnp.clip(jax.random.normal(jax.random.fold_in(key, 21), array_shape, jnp.float32), -6.0, 6.0)


def draw_kv_blocks(key, part):
    return block_tables(key)[0]


def draw_block_counts(key, part):
    return block_tables(key)[1]


def draw_keys(key, part):
    field_draw = key_field(key)
    return field_draw.astype(jnp.bfloat16)


def draw_queries(key, part):
    array_shape = (FRAMES * FTOK, HEADS * HD)
    return jnp.clip(2.0 * jax.random.normal(jax.random.fold_in(key, 22), array_shape, jnp.float32), -12.0, 12.0).astype(jnp.bfloat16)


def shard_levels(rng, extent, pieces, smallest, top_value):
    def one(axis_at, blocks):
        steps = jax.random.uniform(jax.random.fold_in(jax.random.fold_in(rng, 6), axis_at), (blocks,), jnp.float32, smallest / len(pieces), top_value / len(pieces))
        return jnp.repeat(jnp.exp(steps), extent[axis_at] // blocks).reshape((-1,) + (1,) * (len(extent) - axis_at - 1))

    loudness = one(*pieces[0])
    for cut in pieces[1:]:
        loudness = loudness * one(*cut)
    return loudness


def gaussian(stream_key, dims, deviation, most, shards=(), kind=jnp.bfloat16):
    array = deviation * jax.random.normal(stream_key, dims, jnp.float32)
    if shards:
        array = array * shard_levels(stream_key, dims, shards, -0.22, 0.18)
    return jnp.clip(array, -most, most).astype(kind)


def setup_inputs(seed: int = 0) -> dict:
    key_of = jax.random.split(jax.random.key(seed), 6)
    queries = draw_queries(jax.random.fold_in(key_of[5], 71), 0)
    keys = draw_keys(jax.random.fold_in(key_of[5], 71), 0)
    values = gaussian(key_of[2], (TOKENS, D), 1.0, 6.0, ((0, 32),))
    kv_blocks = draw_kv_blocks(jax.random.fold_in(key_of[5], 71), 0)
    block_counts = draw_block_counts(jax.random.fold_in(key_of[5], 71), 0)
    return dict(queries=queries, keys=keys, values=values, kv_blocks=kv_blocks, block_counts=block_counts)


NEG_FILL = -1.0e30


def rotate_time(matrix, frame_ids):
    row_count = matrix.shape[0]
    head_count = matrix.shape[1] // HD
    per_head = matrix.reshape(row_count, head_count, HD)
    pair_index = jnp.arange(8, dtype=jnp.float32)
    frequency = 256.0 ** (-pair_index / 8.0)
    angles = frame_ids.astype(jnp.float32)[:, None] * frequency[None, :]
    cosine = jnp.cos(angles)[:, None, :]
    sine_part = jnp.sin(angles)[:, None, :]
    pair_view = per_head[:, :, :16].reshape(row_count, head_count, 8, 2)
    even_part = pair_view[..., 0]
    odd_part = pair_view[..., 1]
    turned = jnp.stack([even_part * cosine - odd_part * sine_part, even_part * sine_part + odd_part * cosine], axis=-1)
    joined = jnp.concatenate([turned.reshape(row_count, head_count, 16), per_head[:, :, 16:]], axis=2)
    return joined.reshape(row_count, head_count * HD)


def signed_distances(frame_count):
    base = [1, 2, 3]
    power = 4
    while power < frame_count:
        base.append(power)
        power = power * 2
    result = [0]
    for step in base:
        result.append(step)
        result.append(-step)
    return result


def slot_cap(distance):
    if distance == 0:
        return SLOTS
    if abs(distance) == 1:
        return 2
    return 1


def frame_partial(query_group, picked_keys, picked_values, valid_counts, cap):
    scores = jnp.einsum("bqhd,bskhd->bhqsk", query_group, picked_keys.astype(jnp.float32)) * (HD ** -0.5)
    usable = (jnp.arange(cap, dtype=jnp.int32)[None, :] < valid_counts[:, None])[:, None, None, :, None]
    masked = jnp.where(usable, scores, NEG_FILL)
    part_max = jnp.max(masked, axis=(3, 4))
    probs = jnp.where(usable, jnp.exp(masked - part_max[..., None, None]), 0.0)
    part_sum = jnp.sum(probs, axis=(3, 4))
    probs_low = lax.optimization_barrier(probs.astype(jnp.bfloat16)).astype(jnp.float32)
    part_num = jnp.einsum("bhqsk,bskhd->bqhd", probs_low, picked_values.astype(jnp.float32))
    part_num = lax.optimization_barrier(part_num.astype(jnp.bfloat16)).astype(jnp.float32)
    return part_num, part_max, part_sum


def merge_state(state, part):
    run_max, run_sum, run_num = state
    part_num, part_max, part_sum = part
    new_max = jnp.maximum(run_max, part_max)
    old_scale = jnp.exp(run_max - new_max)
    new_scale = jnp.exp(part_max - new_max)
    run_sum = old_scale * run_sum + new_scale * part_sum
    run_num = run_num * jnp.transpose(old_scale, (0, 2, 1))[..., None] + part_num * jnp.transpose(new_scale, (0, 2, 1))[..., None]
    return new_max, run_sum, run_num


def reference(queries, keys, values, kv_blocks, block_counts):
    frame_blocks = FTOK // BLK
    row_frames = jnp.arange(TOKENS, dtype=jnp.int32) // FTOK
    query_turned = rotate_time(queries.astype(jnp.float32), row_frames).astype(jnp.bfloat16)
    key_turned = rotate_time(keys.astype(jnp.float32), row_frames).astype(jnp.bfloat16)
    query_all = query_turned.reshape(FRAMES, frame_blocks, BLK, HEADS, HD)
    key_blocks = key_turned.reshape(FRAMES * frame_blocks, BLK, HEADS, HD)
    value_blocks = values.reshape(FRAMES * frame_blocks, BLK, HEADS, HD)

    def one_frame(frame):
        query_group = query_all[frame].astype(jnp.float32)
        state = (jnp.full((frame_blocks, HEADS, BLK), NEG_FILL, jnp.float32), jnp.zeros((frame_blocks, HEADS, BLK), jnp.float32), jnp.zeros((frame_blocks, BLK, HEADS, HD), jnp.float32))
        for distance in signed_distances(FRAMES):
            cap = slot_cap(distance)
            source = frame - distance
            valid = (source >= 0) & (source < FRAMES)
            source_clip = jnp.clip(source, 0, FRAMES - 1).astype(jnp.int32)
            row_start = (frame * frame_blocks).astype(jnp.int32)
            block_ids = lax.dynamic_slice(kv_blocks, (row_start, (source_clip * SLOTS).astype(jnp.int32)), (frame_blocks, cap))
            counts = lax.dynamic_slice(block_counts, (row_start, source_clip), (frame_blocks, 1))[:, 0]
            counts = jnp.where(valid, counts, 0)
            part = frame_partial(query_group, key_blocks[block_ids], value_blocks[block_ids], counts, cap)
            state = merge_state(state, part)
        denominator = jnp.transpose(state[1], (0, 2, 1))[..., None]
        return state[2] / denominator

    result = lax.map(one_frame, jnp.arange(FRAMES, dtype=jnp.int32))
    return result.reshape(TOKENS, D).astype(jnp.bfloat16)
```

```python
import functools
import math

import jax
import jax.numpy as jnp
import numpy as np
from jax import lax
from jax.experimental import pallas as pl
from jax.experimental.pallas import tpu as pltpu
from jax.sharding import PartitionSpec as P

HD = 128
BLK = 128
SLOTS = 4
MESH = pl.DeviceIdType.MESH
EXP2_SCALE = HD ** (-0.5) * math.log2(math.e)


def turn_table(frames):
    lane = np.arange(HD)
    frequency = (256.0 ** (-(lane // 2) / 8.0)).astype(np.float32)
    angle = np.arange(frames, dtype=np.float32)[:, None] * frequency[None, :]
    cosine = np.cos(angle.astype(np.float64))
    sine = np.sin(angle.astype(np.float64))
    turned = lane < 16
    even = lane % 2 == 0
    table = np.zeros((frames, 8, HD), np.float32)
    table[:, 0] = np.where(turned, cosine, 1.0)
    table[:, 1] = np.where(turned & even, -sine, 0.0)
    table[:, 2] = np.where(turned & ~even, sine, 0.0)
    return table


def chunk_sizes(heads):
    if heads < 6:
        return (1,) * heads
    middle = heads - 6
    rest = (middle % 3,) if middle % 3 else ()
    return (1, 2) + (3,) * (middle // 3) + rest + (2, 1)


def source_names(frames):
    names = ["own", "S", "X", "XS", "Zm", "Zp", "ZS", "ZX", "ZXS"]
    power = 8
    while power < frames:
        names += ["P%d" % power] if power * 2 >= frames else ["M%d" % power, "P%d" % power]
        power = power * 2
    return names


def kernel(plan, kv_ref, count_ref, turn_ref, q_hbm, k_hbm, v_hbm, out_hbm, *scratch):
    frames, groups, rows, heads, sizes, names = plan
    chunks = len(sizes)
    group_width = heads * HD
    widths = [size * HD for size in sizes]
    begins = [sum(widths[:c]) for c in range(chunks)]
    tokens = rows * groups
    frame_blocks = tokens // BLK
    scratch = list(scratch)

    def take(n):
        head, scratch[:] = scratch[:n], scratch[n:]
        return head

    kv = {name: take(chunks) for name in names}
    q_all = take(chunks)
    att = take(chunks)
    q_ref, k_ref, stage_k, stage_q, scores = take(5)
    in_send, in_recv, local_sem, seq_send, seq_recv, out_send, out_recv, out_local, load_sem = take(9)
    where_of = {name: i for i, name in enumerate(names)}

    frame = lax.axis_index("seq")
    me = lax.axis_index("head")
    core = frame % 2
    parity = (frame // 2) % 2
    sibling = frame + 1 - 2 * core
    partner = frame + 2 - 4 * parity
    my_rows = pl.ds(pl.multiple_of(me * rows, rows), rows)
    whole_blocks = rows % BLK == 0
    always = frame >= 0
    even_core, odd_core = core == 0, core == 1
    low, high = parity == 0, parity == 1

    def has(o):
        return frame + o < frames if o > 0 else frame + o >= 0

    side_core = jnp.where(even_core, -4, 4)
    side_pair = jnp.where(low, -4, 4)
    place = {
        "own": frame,
        "S": sibling,
        "X": partner,
        "XS": sibling + partner - frame,
        "Zm": frame - 4,
        "Zp": frame + 4,
        "ZS": sibling + side_core,
        "ZX": partner + side_pair,
        "ZXS": sibling + partner - frame + side_pair,
    }
    for name in names[9:]:
        power = int(name[1:])
        if power * 2 >= frames:
            place[name] = frame + jnp.where(frame >= power, -power, power)
        else:
            place[name] = frame - power if name[0] == "M" else frame + power
    there = {name: (place[name] >= 0) & (place[name] < frames) for name in names}

    def rows_of(buffer, which, group):
        if whole_blocks:
            return buffer.at[which, pl.ds(group * (rows // BLK), rows // BLK)]
        first = group * rows
        return buffer.at[which, first // BLK, pl.ds(pl.multiple_of(first % BLK, rows), rows), :]

    steps = [4]
    while steps[-1] * 4 < frames:
        steps.append(steps[-1] * 2)

    load_k = pltpu.make_async_copy(k_hbm, k_ref, load_sem.at[0])
    load_q = pltpu.make_async_copy(q_hbm, q_ref, load_sem.at[1])

    barrier = pltpu.get_barrier_semaphore()

    def greet(seq, head):
        pl.semaphore_signal(barrier, inc=1, device_id=(seq, head), device_id_type=MESH)

    expected = 2 + groups - 1
    for s in steps:
        for o in (-s, s):
            @pl.when(has(o))
            def _(o=o):
                greet(frame + o, me)

            expected = expected + jnp.where(has(o), 1, 0)
    greet(partner, me)
    for r in range(1, groups):
        greet(frame, (me + r) % groups)
    greet(sibling, me)

    def turn(src, dst, column, c, blocked):
        table = turn_ref[frame]
        cosine, up, down = table[0:1, :], table[1:2, :], table[2:3, :]
        piece = min(rows, 32)

        @pl.loop(0, rows // piece)
        def _(i):
            at = pl.ds(pl.multiple_of(i * piece, piece), piece)
            for h in range(sizes[c]):
                col = pl.ds(pl.multiple_of(column + h * HD, HD), HD)
                x = src[at, col].astype(jnp.float32)
                y = x * cosine + pltpu.roll(x, HD - 1, 1) * up + pltpu.roll(x, 1, 1) * down
                y = y.astype(jnp.bfloat16)
                lanes = slice(h * HD, (h + 1) * HD)
                if blocked and whole_blocks:
                    inner = pl.ds(pl.multiple_of(i * piece % BLK, piece), piece)
                    dst[i * piece // BLK, inner, lanes] = y
                else:
                    dst[at, lanes] = y

    def column_of(group, c):
        return pl.multiple_of(group * group_width + begins[c], HD)

    def staged(buffer, r, c, blocked):
        col = pl.ds(begins[c], widths[c])
        return buffer.at[r - 1, :, :, col] if blocked and whole_blocks else buffer.at[r - 1, :, col]

    def value_columns(group, c):
        col = pl.ds(column_of(group, c), widths[c])
        return v_hbm.at[:, :, col] if whole_blocks else v_hbm.at[:, col]

    def in_copy(c, r, what):
        target = (me + r) % groups
        if what == 0:
            src = staged(stage_k, r, c, True)
        elif what == 1:
            src = value_columns(target, c)
        else:
            src = staged(stage_q, r, c, False)
        dst = q_all[c].at[my_rows, :] if what == 2 else rows_of(kv["own"][c], what, me)
        return pltpu.make_async_remote_copy(
            src_ref=src, dst_ref=dst, send_sem=in_send.at[c, r - 1, what],
            recv_sem=in_recv.at[c, r - 1, what], device_id=(frame, target), device_id_type=MESH)

    def in_wait(c, r, what):
        source = (me + groups - r) % groups
        at = pl.ds(pl.multiple_of(source * rows, rows), rows)
        dst = q_all[c].at[at, :] if what == 2 else rows_of(kv["own"][c], what, source)
        pltpu.make_async_remote_copy(
            src_ref=dst, dst_ref=dst, send_sem=in_send.at[c, r - 1, what],
            recv_sem=in_recv.at[c, r - 1, what], device_id=(frame, source),
            device_id_type=MESH).wait_recv()

    def local_value(c):
        return pltpu.make_async_copy(
            value_columns(me, c), rows_of(kv["own"][c], 1, me), local_sem.at[c])

    own_routes = [
        (has(4), "own", "Zm", frame + 4),
        (has(-4), "own", "Zp", frame - 4),
        (always, "own", "X", partner),
        (always, "own", "S", sibling),
    ]
    after_z = []
    if 8 < frames:
        into = ("P8", "P8") if 16 >= frames else ("M8", "P8")
        after_z += [
            (has(-4) & has(4), "Zm", into[0], frame + 4),
            (has(-4) & has(4), "Zp", into[1], frame - 4),
        ]
    after_z += [
        (low & has(4), "Zp", "ZX", partner),
        (high & has(-4), "Zm", "ZX", partner),
        (even_core & has(4), "Zp", "ZS", sibling),
        (odd_core & has(-4), "Zm", "ZS", sibling),
    ]
    after_x = [(always, "X", "XS", sibling)]
    after_zx = [(there["ZX"], "ZX", "ZXS", sibling)]
    after_power = []
    power = 8
    while power * 2 < frames:
        last = power * 4 >= frames
        after_power.append((power, [
            (has(-power) & has(power), "M%d" % power, ("P%d" if last else "M%d") % (2 * power), frame + power),
            (has(-power) & has(power), "P%d" % power, "P%d" % (2 * power), frame - power),
        ]))
        power = power * 2
    routes = own_routes + after_z + after_x + after_zx
    for _, extra in after_power:
        routes = routes + extra
    slot_of = {id(route): i for i, route in enumerate(routes)}

    def whole_copy(c, route):
        _, held, to, target = route
        return pltpu.make_async_remote_copy(
            src_ref=kv[held][c], dst_ref=kv[to][c], send_sem=seq_send.at[c, slot_of[id(route)]],
            recv_sem=seq_recv.at[c, where_of[to]], device_id=(target, me), device_id_type=MESH)

    def send(c, some):
        for route in some:
            @pl.when(route[0])
            def _(route=route):
                whole_copy(c, route).start()

    def send_part(c, which, group):
        for route in own_routes:
            @pl.when(route[0])
            def _(route=route):
                pltpu.make_async_remote_copy(
                    src_ref=rows_of(kv["own"][c], which, group),
                    dst_ref=rows_of(kv[route[2]][c], which, group),
                    send_sem=seq_send.at[c, slot_of[id(route)]],
                    recv_sem=seq_recv.at[c, where_of[route[2]]],
                    device_id=(route[3], me), device_id_type=MESH).start()

    def wait_for(c, name):
        @pl.when(there[name])
        def _():
            pltpu.make_async_remote_copy(
                src_ref=kv[name][c], dst_ref=kv[name][c], send_sem=seq_send.at[c, 0],
                recv_sem=seq_recv.at[c, where_of[name]], device_id=(sibling, me),
                device_id_type=MESH).wait_recv()

    def turn_keys(c):
        for r in range(1, groups):
            turn(k_ref, staged(stage_k, r, c, True), column_of((me + r) % groups, c), c, True)
        turn(k_ref, rows_of(kv["own"][c], 0, me), column_of(me, c), c, True)

    def enter_queries(c):
        for r in range(1, groups):
            turn(q_ref, staged(stage_q, r, c, False), column_of((me + r) % groups, c), c, False)
            in_copy(c, r, 2).start()
        turn(q_ref, q_all[c].at[my_rows, :], column_of(me, c), c, False)

    two = ("S", "XS", "ZXS")
    slots = []
    for name in ["S", "XS"] + [n for n in names if n not in ("own", "S", "XS", "ZXS")] + ["ZXS"]:
        slots += [(name, j) for j in range(2 if name in two else 1)]
    pairs = [slots[i:i + 2] for i in range(0, len(slots), 2)]
    own_pairs = tokens // (2 * BLK)

    def attend(c):
        @pl.loop(0, frame_blocks)
        def _(b):
            at = pl.ds(pl.multiple_of(b * BLK, BLK), BLK)
            table_row = frame * frame_blocks + b
            start = {}
            bound = {}
            for name, j in slots:
                source = jnp.clip(place[name], 0, frames - 1)
                block = kv_ref[table_row, source * SLOTS + j] - source * frame_blocks
                start[name, j] = jnp.clip(block, 0, frame_blocks - 1)
                usable = jnp.where(there[name], count_ref[source, table_row], 0) > j
                bound[name, j] = jnp.where(usable, jnp.float32(jnp.inf), jnp.float32(-jnp.inf))
            for h in range(sizes[c]):
                col = slice(h * HD, (h + 1) * HD)
                query = q_all[c][at, col]

                def side(i, which):
                    if i < own_pairs:
                        return kv["own"][c][which, 2 * i:2 * i + 2, :, col].reshape(2 * BLK, HD)
                    parts = [kv[name][c][which, start[name, j], :, col] for name, j in pairs[i - own_pairs]]
                    return jnp.concatenate(parts, axis=0) if len(parts) > 1 else parts[0]

                top = None
                for i in range(own_pairs + len(pairs)):
                    s = lax.dot_general(query, side(i, 0), (((1,), (1,)), ((), ())),
                                        preferred_element_type=jnp.float32)
                    for k in range(s.shape[1] // BLK):
                        part = s[:, k * BLK:(k + 1) * BLK]
                        if i >= own_pairs:
                            part = jnp.minimum(part, bound[pairs[i - own_pairs][k]])
                        scores[h, i, :, k * BLK:(k + 1) * BLK] = part
                        top = part if top is None else jnp.maximum(top, part)
                top = jnp.max(top, axis=1, keepdims=True)
                total = None
                out = None
                for i in range(own_pairs + len(pairs)):
                    value = side(i, 1)
                    p = jnp.exp2((scores[h, i, :, :value.shape[0]] - top) * EXP2_SCALE)
                    for k in range(p.shape[1] // BLK):
                        part = p[:, k * BLK:(k + 1) * BLK]
                        total = part if total is None else total + part
                    term = jnp.dot(p.astype(jnp.bfloat16), value, preferred_element_type=jnp.float32)
                    out = term if out is None else out + term
                total = jnp.sum(total, axis=1, keepdims=True)
                att[c][at, col] = (out / total).astype(jnp.bfloat16)

    def out_copy(c, r):
        target = (me + r) % groups
        at = pl.ds(pl.multiple_of(target * rows, rows), rows)
        return pltpu.make_async_remote_copy(
            src_ref=att[c].at[at, :], dst_ref=out_hbm.at[:, pl.ds(column_of(me, c), widths[c])],
            send_sem=out_send.at[c, r - 1], recv_sem=out_recv.at[c, r - 1],
            device_id=(frame, target), device_id_type=MESH)

    def out_wait(c, r):
        source = (me + groups - r) % groups
        at = out_hbm.at[:, pl.ds(column_of(source, c), widths[c])]
        pltpu.make_async_remote_copy(
            src_ref=at, dst_ref=at, send_sem=out_send.at[c, r - 1],
            recv_sem=out_recv.at[c, r - 1], device_id=(frame, source),
            device_id_type=MESH).wait_recv()

    def local_out(c):
        return pltpu.make_async_copy(
            att[c].at[my_rows, :], out_hbm.at[:, pl.ds(column_of(me, c), widths[c])], out_local.at[c])

    def leave(c):
        for r in range(1, groups):
            out_copy(c, r).start()
        local_out(c).start()

    load_k.start()
    for c in range(chunks):
        local_value(c).start()
    load_q.start()
    load_k.wait()
    turn_keys(0)
    pl.semaphore_wait(barrier, expected)

    for c in range(chunks):
        for r in range(1, groups):
            in_copy(c, r, 1).start()
        local_value(c).wait()
        send_part(c, 1, me)
        if c > 0:
            turn_keys(c)
        for r in range(1, groups):
            in_copy(c, r, 0).start()
        send_part(c, 0, me)
    load_q.wait()
    for c in range(chunks):
        enter_queries(c)
    for name in names:
        if name in ("own", "S", "X", "XS"):
            continue

        @pl.when(jnp.logical_not(there[name]))
        def _(name=name):
            @pl.loop(0, frame_blocks)
            def _(i):
                for c in range(chunks):
                    for which in range(2):
                        kv[name][c][which, i] = jnp.zeros((BLK, widths[c]), jnp.bfloat16)

    for c in range(chunks):
        for r in range(1, groups):
            for which in (1, 0):
                in_wait(c, r, which)
                send_part(c, which, (me + groups - r) % groups)
    for c in range(chunks):
        wait_for(c, "Zm")
        wait_for(c, "Zp")
        send(c, after_z)
        wait_for(c, "X")
        send(c, after_x)
    for c in range(chunks):
        wait_for(c, "ZX")
        send(c, after_zx)
        for power, some in after_power:
            wait_for(c, "M%d" % power)
            wait_for(c, "P%d" % power)
            send(c, some)
        if len(names) > 9:
            wait_for(c, names[-1])
        for name in ("S", "XS", "ZS", "ZXS"):
            wait_for(c, name)
        for r in range(1, groups):
            in_wait(c, r, 2)
        attend(c)
        leave(c)

    for c in range(chunks):
        for r in range(1, groups):
            for what in range(3):
                in_copy(c, r, what).wait_send()
            out_copy(c, r).wait_send()
            out_wait(c, r)
        local_out(c).wait()
        for route in routes:
            @pl.when(route[0])
            def _(route=route):
                whole_copy(c, route).wait_send()


def local(queries, keys, values, kv_blocks, block_counts):
    frames = lax.axis_size("seq")
    groups = lax.axis_size("head")
    rows, model = queries.shape
    heads = model // HD // groups
    sizes = chunk_sizes(heads)
    chunks = len(sizes)
    tokens = rows * groups
    names = source_names(frames)
    n_pairs = tokens // (2 * BLK) + (len(names) + 3) // 2
    plan = (frames, groups, rows, heads, sizes, tuple(names))
    n_routes = 10 + 2 * len(names)
    lead = (rows // BLK, BLK) if rows % BLK == 0 else (rows,)
    blocks = [pltpu.VMEM((2, tokens // BLK, BLK, size * HD), jnp.bfloat16) for size in sizes]
    flats = [pltpu.VMEM((tokens, size * HD), jnp.bfloat16) for size in sizes]
    group_width = heads * HD
    whole = pltpu.VMEM((rows, model), jnp.bfloat16)
    stage_q = pltpu.VMEM((max(groups - 1, 1), rows, group_width), jnp.bfloat16)
    stage_k = pltpu.VMEM((max(groups - 1, 1),) + lead + (group_width,), jnp.bfloat16)
    sem = pltpu.SemaphoreType.DMA
    others = max(groups - 1, 1)
    return pl.pallas_call(
        functools.partial(kernel, plan),
        out_shape=jax.ShapeDtypeStruct((rows, model), jnp.bfloat16),
        in_specs=[
            pl.BlockSpec(memory_space=pltpu.SMEM),
            pl.BlockSpec(memory_space=pltpu.SMEM),
            pl.BlockSpec(memory_space=pltpu.VMEM),
            pl.BlockSpec(memory_space=pl.ANY),
            pl.BlockSpec(memory_space=pl.ANY),
            pl.BlockSpec(memory_space=pl.ANY),
        ],
        out_specs=pl.BlockSpec(memory_space=pl.ANY),
        scratch_shapes=blocks * len(names) + flats * 2 + [
            whole,
            whole,
            stage_k,
            stage_q,
            pltpu.VMEM((max(sizes), n_pairs, BLK, 2 * BLK), jnp.float32),
            sem((chunks, others, 3)),
            sem((chunks, others, 3)),
            sem((chunks,)),
            sem((chunks, n_routes)),
            sem((chunks, len(names))),
            sem((chunks, others)),
            sem((chunks, others)),
            sem((chunks,)),
            sem((2,)),
        ],
        compiler_params=pltpu.CompilerParams(
            collective_id=0, has_side_effects=True, vmem_limit_bytes=60 * 1024 * 1024
        ),
    )(kv_blocks, block_counts.T, jnp.asarray(turn_table(frames)), queries, keys,
      values.reshape(lead + (model,)))


def solution(mesh):
    in_specs = (
        P(("seq", "head"), None),
        P(("seq", "head"), None),
        P(("seq", "head"), None),
        P(),
        P(),
    )
    out_specs = P(("seq", "head"), None)
    return jax.shard_map(local, mesh=mesh, in_specs=in_specs, out_specs=out_specs, check_vma=False)
```

```python
import functools
import math

import jax
import jax.numpy as jnp
import numpy as np
from jax import lax
from jax.experimental import pallas as pl
from jax.experimental.pallas import tpu as pltpu
from jax.sharding import PartitionSpec as P

HD = 128
BLK = 128
SLOTS = 4
TWO_PASS = 2
MESH = pl.DeviceIdType.MESH
EXP2_SCALE = HD ** (-0.5) * math.log2(math.e)


def turn_table(frames):
    lane = np.arange(HD)
    frequency = (256.0 ** (-(lane // 2) / 8.0)).astype(np.float32)
    angle = np.arange(frames, dtype=np.float32)[:, None] * frequency[None, :]
    cosine = np.cos(angle.astype(np.float64))
    sine = np.sin(angle.astype(np.float64))
    turned = lane < 16
    even = lane % 2 == 0
    table = np.zeros((frames, 8, HD), np.float32)
    table[:, 0] = np.where(turned, cosine, 1.0)
    table[:, 1] = np.where(turned & even, -sine, 0.0)
    table[:, 2] = np.where(turned & ~even, sine, 0.0)
    return table


def chunk_sizes(heads):
    if heads < 6:
        return (1,) * heads
    middle = heads - 6
    rest = (middle % 3,) if middle % 3 else ()
    return (1, 2) + (3,) * (middle // 3) + rest + (2, 1)


def source_names(frames):
    names = ["own", "S", "X", "XS", "Zm", "Zp", "ZS", "ZX", "ZXS"]
    power = 8
    while power < frames:
        names += ["P%d" % power] if power * 2 >= frames else ["M%d" % power, "P%d" % power]
        power = power * 2
    return names


def kernel(plan, kv_hbm, count_hbm, turn_hbm, q_hbm, k_hbm, v_hbm, out_hbm, *scratch):
    frames, groups, rows, heads, sizes, names = plan
    chunks = len(sizes)
    one_pass = max(chunks - TWO_PASS, 0)
    kept_from = sum(sizes[:one_pass])
    group_width = heads * HD
    widths = [size * HD for size in sizes]
    begins = [sum(widths[:c]) for c in range(chunks)]
    tokens = rows * groups
    frame_blocks = tokens // BLK
    scratch = list(scratch)

    def take(n):
        head, scratch[:] = scratch[:n], scratch[n:]
        return head

    kv = {name: take(chunks) for name in names}
    q_all = take(chunks)
    att = take(chunks)
    kv_ref, count_ref, turn_ref = take(3)
    q_ref, k_ref, stage_k, stage_q, scores, tops, sums, numerators = take(8)
    in_send, in_recv, local_sem, seq_send, seq_recv, out_send, out_recv, out_local, load_sem = take(9)
    where_of = {name: i for i, name in enumerate(names)}

    frame = lax.axis_index("seq")
    me = lax.axis_index("head")
    core = frame % 2
    parity = (frame // 2) % 2
    sibling = frame + 1 - 2 * core
    partner = frame + 2 - 4 * parity
    my_rows = pl.ds(pl.multiple_of(me * rows, rows), rows)
    whole_blocks = rows % BLK == 0
    always = frame >= 0
    even_core, odd_core = core == 0, core == 1
    low, high = parity == 0, parity == 1

    def has(o):
        return frame + o < frames if o > 0 else frame + o >= 0

    side_core = jnp.where(even_core, -4, 4)
    side_pair = jnp.where(low, -4, 4)
    place = {
        "own": frame,
        "S": sibling,
        "X": partner,
        "XS": sibling + partner - frame,
        "Zm": frame - 4,
        "Zp": frame + 4,
        "ZS": sibling + side_core,
        "ZX": partner + side_pair,
        "ZXS": sibling + partner - frame + side_pair,
    }
    for name in names[9:]:
        power = int(name[1:])
        if power * 2 >= frames:
            place[name] = frame + jnp.where(frame >= power, -power, power)
        else:
            place[name] = frame - power if name[0] == "M" else frame + power
    there = {name: (place[name] >= 0) & (place[name] < frames) for name in names}

    def rows_of(buffer, which, group):
        if whole_blocks:
            return buffer.at[which, pl.ds(group * (rows // BLK), rows // BLK)]
        first = group * rows
        return buffer.at[which, first // BLK, pl.ds(pl.multiple_of(first % BLK, rows), rows), :]

    steps = [4]
    while steps[-1] * 4 < frames:
        steps.append(steps[-1] * 2)

    load_k = pltpu.make_async_copy(k_hbm, k_ref, load_sem.at[0])
    load_q = pltpu.make_async_copy(q_hbm, q_ref, load_sem.at[1])
    load_turn = pltpu.make_async_copy(turn_hbm.at[frame], turn_ref, load_sem.at[2])
    load_kv = pltpu.make_async_copy(kv_hbm, kv_ref, load_sem.at[3])
    load_count = pltpu.make_async_copy(count_hbm, count_ref, load_sem.at[4])
    load_turn.start()
    load_k.start()

    barrier = pltpu.get_barrier_semaphore()

    def greet(seq, head):
        pl.semaphore_signal(barrier, inc=1, device_id=(seq, head), device_id_type=MESH)

    expected = 2 + groups - 1
    for s in steps:
        for o in (-s, s):
            @pl.when(has(o))
            def _(o=o):
                greet(frame + o, me)

            expected = expected + jnp.where(has(o), 1, 0)
    greet(partner, me)
    for r in range(1, groups):
        greet(frame, (me + r) % groups)
    greet(sibling, me)

    def turn(src, dst, column, c, blocked):
        cosine, up, down = turn_ref[0:1, :], turn_ref[1:2, :], turn_ref[2:3, :]
        piece = min(rows, 32)

        @pl.loop(0, rows // piece)
        def _(i):
            at = pl.ds(pl.multiple_of(i * piece, piece), piece)
            for h in range(sizes[c]):
                col = pl.ds(pl.multiple_of(column + h * HD, HD), HD)
                x = src[at, col].astype(jnp.float32)
                y = x * cosine + pltpu.roll(x, HD - 1, 1) * up + pltpu.roll(x, 1, 1) * down
                y = y.astype(jnp.bfloat16)
                lanes = slice(h * HD, (h + 1) * HD)
                if blocked and whole_blocks:
                    inner = pl.ds(pl.multiple_of(i * piece % BLK, piece), piece)
                    dst[i * piece // BLK, inner, lanes] = y
                else:
                    dst[at, lanes] = y

    def column_of(group, c):
        return pl.multiple_of(group * group_width + begins[c], HD)

    def staged(buffer, r, c, blocked):
        col = pl.ds(begins[c], widths[c])
        return buffer.at[r - 1, :, :, col] if blocked and whole_blocks else buffer.at[r - 1, :, col]

    def value_columns(group, c):
        col = pl.ds(column_of(group, c), widths[c])
        return v_hbm.at[:, :, col] if whole_blocks else v_hbm.at[:, col]

    def in_copy(c, r, what):
        target = (me + r) % groups
        if what == 0:
            src = staged(stage_k, r, c, True)
        elif what == 1:
            src = value_columns(target, c)
        else:
            src = staged(stage_q, r, c, False)
        dst = q_all[c].at[my_rows, :] if what == 2 else rows_of(kv["own"][c], what, me)
        return pltpu.make_async_remote_copy(
            src_ref=src, dst_ref=dst, send_sem=in_send.at[c, r - 1, what],
            recv_sem=in_recv.at[c, r - 1, what], device_id=(frame, target), device_id_type=MESH)

    def in_wait(c, r, what):
        source = (me + groups - r) % groups
        at = pl.ds(pl.multiple_of(source * rows, rows), rows)
        dst = q_all[c].at[at, :] if what == 2 else rows_of(kv["own"][c], what, source)
        pltpu.make_async_remote_copy(
            src_ref=dst, dst_ref=dst, send_sem=in_send.at[c, r - 1, what],
            recv_sem=in_recv.at[c, r - 1, what], device_id=(frame, source),
            device_id_type=MESH).wait_recv()

    def local_value(c):
        return pltpu.make_async_copy(
            value_columns(me, c), rows_of(kv["own"][c], 1, me), local_sem.at[c])

    own_routes = [
        (has(4), "own", "Zm", frame + 4),
        (has(-4), "own", "Zp", frame - 4),
        (always, "own", "X", partner),
        (always, "own", "S", sibling),
    ]
    after_z = []
    if 8 < frames:
        into = ("P8", "P8") if 16 >= frames else ("M8", "P8")
        after_z += [
            (has(-4) & has(4), "Zm", into[0], frame + 4),
            (has(-4) & has(4), "Zp", into[1], frame - 4),
        ]
    after_z += [
        (low & has(4), "Zp", "ZX", partner),
        (high & has(-4), "Zm", "ZX", partner),
        (even_core & has(4), "Zp", "ZS", sibling),
        (odd_core & has(-4), "Zm", "ZS", sibling),
    ]
    after_x = [(always, "X", "XS", sibling)]
    after_zx = [(there["ZX"], "ZX", "ZXS", sibling)]
    after_power = []
    power = 8
    while power * 2 < frames:
        last = power * 4 >= frames
        after_power.append((power, [
            (has(-power) & has(power), "M%d" % power, ("P%d" if last else "M%d") % (2 * power), frame + power),
            (has(-power) & has(power), "P%d" % power, "P%d" % (2 * power), frame - power),
        ]))
        power = power * 2
    routes = own_routes + after_z + after_x + after_zx
    for _, extra in after_power:
        routes = routes + extra
    slot_of = {id(route): i for i, route in enumerate(routes)}

    def whole_copy(c, route):
        _, held, to, target = route
        return pltpu.make_async_remote_copy(
            src_ref=kv[held][c], dst_ref=kv[to][c], send_sem=seq_send.at[c, slot_of[id(route)]],
            recv_sem=seq_recv.at[c, where_of[to]], device_id=(target, me), device_id_type=MESH)

    def send(c, some):
        for route in some:
            @pl.when(route[0])
            def _(route=route):
                whole_copy(c, route).start()

    def send_part(c, which, group):
        for route in own_routes:
            @pl.when(route[0])
            def _(route=route):
                pltpu.make_async_remote_copy(
                    src_ref=rows_of(kv["own"][c], which, group),
                    dst_ref=rows_of(kv[route[2]][c], which, group),
                    send_sem=seq_send.at[c, slot_of[id(route)]],
                    recv_sem=seq_recv.at[c, where_of[route[2]]],
                    device_id=(route[3], me), device_id_type=MESH).start()

    def wait_for(c, name):
        @pl.when(there[name])
        def _():
            pltpu.make_async_remote_copy(
                src_ref=kv[name][c], dst_ref=kv[name][c], send_sem=seq_send.at[c, 0],
                recv_sem=seq_recv.at[c, where_of[name]], device_id=(sibling, me),
                device_id_type=MESH).wait_recv()

    def turn_keys(c):
        for r in range(1, groups):
            turn(k_ref, staged(stage_k, r, c, True), column_of((me + r) % groups, c), c, True)
        turn(k_ref, rows_of(kv["own"][c], 0, me), column_of(me, c), c, True)

    def enter_queries(c):
        for r in range(1, groups):
            turn(q_ref, staged(stage_q, r, c, False), column_of((me + r) % groups, c), c, False)
            in_copy(c, r, 2).start()
        turn(q_ref, q_all[c].at[my_rows, :], column_of(me, c), c, False)

    two = ("S", "XS", "ZXS")
    early_names = ("S", "XS", "X", "Zm", "Zp", "ZS")
    late_names = [n for n in names if n not in early_names + ("own", "ZXS")] + ["ZXS"]

    def paired(some):
        slots = [(name, j) for name in some for j in range(2 if name in two else 1)]
        return [slots[i:i + 2] for i in range(0, len(slots), 2)]

    own_groups = [[("own", 2 * i), ("own", 2 * i + 1)] for i in range(tokens // (2 * BLK))]
    early, late = paired(early_names), paired(late_names)

    def attend(c, units, begin, finish, first, count):
        @pl.loop(0, count)
        def _(i):
            b = first + i
            at = pl.ds(pl.multiple_of(b * BLK, BLK), BLK)
            table_row = frame * frame_blocks + b
            start = {}
            bound = {}
            for name, j in [slot for unit in units for slot in unit if slot[0] != "own"]:
                source = jnp.clip(place[name], 0, frames - 1)
                block = kv_ref[table_row, source * SLOTS + j] - source * frame_blocks
                start[name, j] = jnp.clip(block, 0, frame_blocks - 1)
                usable = jnp.where(there[name], count_ref[source, table_row], 0) > j
                bound[name, j] = jnp.where(usable, jnp.float32(jnp.inf), jnp.float32(-jnp.inf))
            for h in range(sizes[c]):
                col = slice(h * HD, (h + 1) * HD)
                query = q_all[c][at, col]
                kept = begins[c] // HD + h - kept_from

                def side(unit, which):
                    name, j = unit[0]
                    if name == "own":
                        return kv[name][c][which, j:j + 2, :, col].reshape(2 * BLK, HD)
                    parts = [kv[name][c][which, start[name, j], :, col] for name, j in unit]
                    return jnp.concatenate(parts, axis=0) if len(parts) > 1 else parts[0]

                top = None if begin else tops[kept, b]
                for u, unit in enumerate(units):
                    s = lax.dot_general(query, side(unit, 0), (((1,), (1,)), ((), ())),
                                        preferred_element_type=jnp.float32)
                    for k, slot in enumerate(unit):
                        part = s[:, k * BLK:(k + 1) * BLK]
                        if slot[0] != "own":
                            part = jnp.minimum(part, bound[slot])
                        scores[h, u, :, k * BLK:(k + 1) * BLK] = part
                        top = part if top is None else jnp.maximum(top, part)
                top = jnp.max(top, axis=1, keepdims=True)
                if begin:
                    total = None
                    out = None
                else:
                    factor = jnp.exp2((tops[kept, b] - top) * EXP2_SCALE)
                    total = sums[kept, b] * factor
                    out = numerators[kept, b] * factor
                for u, unit in enumerate(units):
                    p = jnp.exp2((scores[h, u, :, :len(unit) * BLK] - top) * EXP2_SCALE)
                    for k in range(len(unit)):
                        part = p[:, k * BLK:(k + 1) * BLK]
                        total = part if total is None else total + part
                    term = jnp.dot(p.astype(jnp.bfloat16), side(unit, 1), preferred_element_type=jnp.float32)
                    out = term if out is None else out + term
                if finish:
                    total = jnp.sum(total, axis=1, keepdims=True)
                    att[c][at, col] = (out / total).astype(jnp.bfloat16)
                else:
                    tops[kept, b] = jnp.broadcast_to(top, (BLK, BLK))
                    sums[kept, b] = total
                    numerators[kept, b] = out

    def out_copy(c, r):
        target = (me + r) % groups
        at = pl.ds(pl.multiple_of(target * rows, rows), rows)
        return pltpu.make_async_remote_copy(
            src_ref=att[c].at[at, :], dst_ref=out_hbm.at[:, pl.ds(column_of(me, c), widths[c])],
            send_sem=out_send.at[c, r - 1], recv_sem=out_recv.at[c, r - 1],
            device_id=(frame, target), device_id_type=MESH)

    def out_wait(c, r):
        source = (me + groups - r) % groups
        at = out_hbm.at[:, pl.ds(column_of(source, c), widths[c])]
        pltpu.make_async_remote_copy(
            src_ref=at, dst_ref=at, send_sem=out_send.at[c, r - 1],
            recv_sem=out_recv.at[c, r - 1], device_id=(frame, source),
            device_id_type=MESH).wait_recv()

    def local_out(c):
        return pltpu.make_async_copy(
            att[c].at[my_rows, :], out_hbm.at[:, pl.ds(column_of(me, c), widths[c])], out_local.at[c])

    def leave(c):
        for r in range(1, groups):
            out_copy(c, r).start()
        local_out(c).start()

    for c in range(chunks):
        local_value(c).start()
    load_q.start()
    load_kv.start()
    load_count.start()
    load_turn.wait()
    load_k.wait()
    turn_keys(0)
    pl.semaphore_wait(barrier, expected)

    for c in range(chunks):
        for r in range(1, groups):
            in_copy(c, r, 1).start()
        local_value(c).wait()
        send_part(c, 1, me)
        if c > 0:
            turn_keys(c)
        for r in range(1, groups):
            in_copy(c, r, 0).start()
        send_part(c, 0, me)
    load_q.wait()
    load_kv.wait()
    load_count.wait()
    for c in range(chunks):
        enter_queries(c)
    for name in names:
        if name in ("own", "S", "X", "XS"):
            continue

        @pl.when(jnp.logical_not(there[name]))
        def _(name=name):
            @pl.loop(0, frame_blocks)
            def _(i):
                for c in range(chunks):
                    for which in range(2):
                        kv[name][c][which, i] = jnp.zeros((BLK, widths[c]), jnp.bfloat16)

    for c in range(chunks):
        for r in range(1, groups):
            for which in (1, 0):
                in_wait(c, r, which)
                send_part(c, which, (me + groups - r) % groups)
    for c in range(chunks):
        wait_for(c, "Zm")
        wait_for(c, "Zp")
        send(c, after_z)
        wait_for(c, "X")
        send(c, after_x)
    for c in range(one_pass, chunks):
        for name in ("S", "XS", "ZS"):
            wait_for(c, name)
        for r in range(1, groups):
            in_wait(c, r, 2)
        attend(c, own_groups + early, True, False, 0, frame_blocks)

    def drain_out(c):
        for r in range(1, groups):
            out_copy(c, r).wait_send()
            out_wait(c, r)
        local_out(c).wait()

    for c in range(chunks):
        wait_for(c, "ZX")
        send(c, after_zx)
        for power, some in after_power:
            wait_for(c, "M%d" % power)
            wait_for(c, "P%d" % power)
            send(c, some)
        if c == chunks - 1:
            for d in range(chunks):
                for r in range(1, groups):
                    for what in range(3):
                        in_copy(d, r, what).wait_send()
            for route in routes:
                @pl.when(route[0])
                def _(route=route):
                    for d in range(chunks - 1):
                        whole_copy(d, route).wait_send()
            for d in range(chunks - 2):
                drain_out(d)
        if len(names) > 9:
            wait_for(c, names[-1])
        for name in ("S", "XS", "ZS", "ZXS") if c < one_pass else ("ZXS",):
            wait_for(c, name)
        for r in range(1, groups):
            if c < one_pass:
                in_wait(c, r, 2)
        if c < one_pass:
            attend(c, own_groups + early + late, True, True, 0, frame_blocks)
            leave(c)
        elif whole_blocks:
            for r in range(1, groups + 1):
                share = rows // BLK
                attend(c, late, False, True, (me + r) % groups * share, share)
                if r < groups:
                    out_copy(c, r).start()
            local_out(c).start()
        else:
            attend(c, late, False, True, 0, frame_blocks)
            leave(c)

    for route in routes:
        @pl.when(route[0])
        def _(route=route):
            whole_copy(chunks - 1, route).wait_send()
    for c in range(max(chunks - 2, 0), chunks):
        drain_out(c)


def local(queries, keys, values, kv_blocks, block_counts):
    frames = lax.axis_size("seq")
    groups = lax.axis_size("head")
    rows, model = queries.shape
    heads = model // HD // groups
    sizes = chunk_sizes(heads)
    chunks = len(sizes)
    tokens = rows * groups
    names = source_names(frames)
    n_pairs = tokens // (2 * BLK) + (len(names) + 4) // 2
    plan = (frames, groups, rows, heads, sizes, tuple(names))
    n_routes = 10 + 2 * len(names)
    lead = (rows // BLK, BLK) if rows % BLK == 0 else (rows,)
    blocks = [pltpu.VMEM((2, tokens // BLK, BLK, size * HD), jnp.bfloat16) for size in sizes]
    flats = [pltpu.VMEM((tokens, size * HD), jnp.bfloat16) for size in sizes]
    group_width = heads * HD
    whole = pltpu.VMEM((rows, model), jnp.bfloat16)
    stage_q = pltpu.VMEM((max(groups - 1, 1), rows, group_width), jnp.bfloat16)
    stage_k = pltpu.VMEM((max(groups - 1, 1),) + lead + (group_width,), jnp.bfloat16)
    state = pltpu.VMEM((sum(sizes[-TWO_PASS:]), tokens // BLK, BLK, HD), jnp.float32)
    sem = pltpu.SemaphoreType.DMA
    others = max(groups - 1, 1)
    return pl.pallas_call(
        functools.partial(kernel, plan),
        out_shape=jax.ShapeDtypeStruct((rows, model), jnp.bfloat16),
        in_specs=[
            pl.BlockSpec(memory_space=pltpu.HBM),
            pl.BlockSpec(memory_space=pltpu.HBM),
            pl.BlockSpec(memory_space=pltpu.HBM),
            pl.BlockSpec(memory_space=pltpu.HBM),
            pl.BlockSpec(memory_space=pltpu.HBM),
            pl.BlockSpec(memory_space=pltpu.HBM),
        ],
        out_specs=pl.BlockSpec(memory_space=pltpu.VMEM),
        scratch_shapes=blocks * len(names) + flats * 2 + [
            pltpu.SMEM(kv_blocks.shape, jnp.int32),
            pltpu.SMEM(block_counts.shape[::-1], jnp.int32),
            pltpu.VMEM((8, HD), jnp.float32),
            whole,
            whole,
            stage_k,
            stage_q,
            pltpu.VMEM((max(sizes), n_pairs, BLK, 2 * BLK), jnp.float32),
            state,
            state,
            state,
            sem((chunks, others, 3)),
            sem((chunks, others, 3)),
            sem((chunks,)),
            sem((chunks, n_routes)),
            sem((chunks, len(names))),
            sem((chunks, others)),
            sem((chunks, others)),
            sem((chunks,)),
            sem((5,)),
        ],
        compiler_params=pltpu.CompilerParams(
            collective_id=0, has_side_effects=True, vmem_limit_bytes=50 * 1024 * 1024
        ),
    )(*[pltpu.with_memory_space_constraint(x, pltpu.HBM) for x in (
        kv_blocks, block_counts.T, jnp.asarray(turn_table(frames)), queries, keys,
        values.reshape(lead + (model,)))])


def solution(mesh):
    in_specs = (
        P(("seq", "head"), None),
        P(("seq", "head"), None),
        P(("seq", "head"), None),
        P(),
        P(),
    )
    out_specs = P(("seq", "head"), None)
    return jax.shard_map(local, mesh=mesh, in_specs=in_specs, out_specs=out_specs, check_vma=False)
```

```python
import functools
import math

import jax
import jax.numpy as jnp
import numpy as np
from jax import lax
from jax.experimental import pallas as pl
from jax.experimental.pallas import tpu as pltpu
from jax.sharding import PartitionSpec as P

HD = 128
BLK = 128
SLOTS = 4
TWO_PASS = 2
MESH = pl.DeviceIdType.MESH
EXP2_SCALE = HD ** (-0.5) * math.log2(math.e)


def turn_table(frames):
    lane = np.arange(HD)
    frequency = (256.0 ** (-(lane // 2) / 8.0)).astype(np.float32)
    angle = np.arange(frames, dtype=np.float32)[:, None] * frequency[None, :]
    cosine = np.cos(angle.astype(np.float64))
    sine = np.sin(angle.astype(np.float64))
    turned = lane < 16
    even = lane % 2 == 0
    table = np.zeros((frames, 8, HD), np.float32)
    table[:, 0] = np.where(turned, cosine, 1.0)
    table[:, 1] = np.where(turned & even, -sine, 0.0)
    table[:, 2] = np.where(turned & ~even, sine, 0.0)
    return table


def chunk_sizes(heads):
    if heads < 6:
        return (1,) * heads
    middle = heads - 6
    rest = (middle % 3,) if middle % 3 else ()
    return (1, 2) + (3,) * (middle // 3) + rest + (2, 1)


def source_names(frames):
    names = ["own", "S", "X", "XS", "Zm", "Zp", "ZS", "ZX", "ZXS"]
    power = 8
    while power < frames:
        names += ["P%d" % power] if power * 2 >= frames else ["M%d" % power, "P%d" % power]
        power = power * 2
    return names


def kernel(plan, kv_hbm, count_hbm, turn_hbm, q_hbm, k_hbm, v_hbm, out_hbm, *scratch):
    frames, groups, rows, heads, sizes, names = plan
    chunks = len(sizes)
    one_pass = max(chunks - TWO_PASS, 0)
    kept_from = sum(sizes[:one_pass])
    group_width = heads * HD
    widths = [size * HD for size in sizes]
    begins = [sum(widths[:c]) for c in range(chunks)]
    tokens = rows * groups
    frame_blocks = tokens // BLK
    scratch = list(scratch)

    def take(n):
        head, scratch[:] = scratch[:n], scratch[n:]
        return head

    kv = {name: take(chunks) for name in names}
    q_all = take(chunks)
    att = take(chunks)
    kv_ref, count_ref, turn_ref = take(3)
    q_ref, k_ref, stage_k, stage_q, scores, tops, sums, numerators = take(8)
    in_send, in_recv, local_sem, seq_send, seq_recv, out_send, out_recv, out_local, load_sem = take(9)
    where_of = {name: i for i, name in enumerate(names)}

    frame = lax.axis_index("seq")
    me = lax.axis_index("head")
    core = frame % 2
    parity = (frame // 2) % 2
    sibling = frame + 1 - 2 * core
    partner = frame + 2 - 4 * parity
    my_rows = pl.ds(pl.multiple_of(me * rows, rows), rows)
    whole_blocks = rows % BLK == 0
    always = frame >= 0
    even_core, odd_core = core == 0, core == 1
    low, high = parity == 0, parity == 1

    def has(o):
        return frame + o < frames if o > 0 else frame + o >= 0

    side_core = jnp.where(even_core, -4, 4)
    side_pair = jnp.where(low, -4, 4)
    place = {
        "own": frame,
        "S": sibling,
        "X": partner,
        "XS": sibling + partner - frame,
        "Zm": frame - 4,
        "Zp": frame + 4,
        "ZS": sibling + side_core,
        "ZX": partner + side_pair,
        "ZXS": sibling + partner - frame + side_pair,
    }
    for name in names[9:]:
        power = int(name[1:])
        if power * 2 >= frames:
            place[name] = frame + jnp.where(frame >= power, -power, power)
        else:
            place[name] = frame - power if name[0] == "M" else frame + power
    there = {name: (place[name] >= 0) & (place[name] < frames) for name in names}

    def rows_of(buffer, which, group):
        if whole_blocks:
            return buffer.at[which, pl.ds(group * (rows // BLK), rows // BLK)]
        first = group * rows
        return buffer.at[which, first // BLK, pl.ds(pl.multiple_of(first % BLK, rows), rows), :]

    steps = [4]
    while steps[-1] * 4 < frames:
        steps.append(steps[-1] * 2)

    load_k = pltpu.make_async_copy(k_hbm, k_ref, load_sem.at[0])
    load_q = pltpu.make_async_copy(q_hbm, q_ref, load_sem.at[1])
    load_turn = pltpu.make_async_copy(turn_hbm.at[frame], turn_ref, load_sem.at[2])
    load_kv = pltpu.make_async_copy(kv_hbm, kv_ref, load_sem.at[3])
    load_count = pltpu.make_async_copy(count_hbm, count_ref, load_sem.at[4])

    barrier = pltpu.get_barrier_semaphore()

    def greet(seq, head):
        pl.semaphore_signal(barrier, inc=1, device_id=(seq, head), device_id_type=MESH)

    expected = 2 + groups - 1
    for s in steps:
        for o in (-s, s):
            @pl.when(has(o))
            def _(o=o):
                greet(frame + o, me)

            expected = expected + jnp.where(has(o), 1, 0)
    greet(partner, me)
    for r in range(1, groups):
        greet(frame, (me + r) % groups)
    greet(sibling, me)
    load_turn.start()
    load_k.start()

    def turn(src, dst, column, c, blocked):
        cosine, up, down = turn_ref[0:1, :], turn_ref[1:2, :], turn_ref[2:3, :]
        piece = min(rows, 32)

        @pl.loop(0, rows // piece)
        def _(i):
            at = pl.ds(pl.multiple_of(i * piece, piece), piece)
            for h in range(sizes[c]):
                col = pl.ds(pl.multiple_of(column + h * HD, HD), HD)
                x = src[at, col].astype(jnp.float32)
                y = x * cosine + pltpu.roll(x, HD - 1, 1) * up + pltpu.roll(x, 1, 1) * down
                y = y.astype(jnp.bfloat16)
                lanes = slice(h * HD, (h + 1) * HD)
                if blocked and whole_blocks:
                    inner = pl.ds(pl.multiple_of(i * piece % BLK, piece), piece)
                    dst[i * piece // BLK, inner, lanes] = y
                else:
                    dst[at, lanes] = y

    def column_of(group, c):
        return pl.multiple_of(group * group_width + begins[c], HD)

    def staged(buffer, r, c, blocked):
        col = pl.ds(begins[c], widths[c])
        return buffer.at[r - 1, :, :, col] if blocked and whole_blocks else buffer.at[r - 1, :, col]

    def value_columns(group, c):
        col = pl.ds(column_of(group, c), widths[c])
        return v_hbm.at[:, :, col] if whole_blocks else v_hbm.at[:, col]

    def in_copy(c, r, what):
        target = (me + r) % groups
        if what == 0:
            src = staged(stage_k, r, c, True)
        elif what == 1:
            src = value_columns(target, c)
        else:
            src = staged(stage_q, r, c, False)
        dst = q_all[c].at[my_rows, :] if what == 2 else rows_of(kv["own"][c], what, me)
        return pltpu.make_async_remote_copy(
            src_ref=src, dst_ref=dst, send_sem=in_send.at[c, r - 1, what],
            recv_sem=in_recv.at[c, r - 1, what], device_id=(frame, target), device_id_type=MESH)

    def in_wait(c, r, what):
        source = (me + groups - r) % groups
        at = pl.ds(pl.multiple_of(source * rows, rows), rows)
        dst = q_all[c].at[at, :] if what == 2 else rows_of(kv["own"][c], what, source)
        pltpu.make_async_remote_copy(
            src_ref=dst, dst_ref=dst, send_sem=in_send.at[c, r - 1, what],
            recv_sem=in_recv.at[c, r - 1, what], device_id=(frame, source),
            device_id_type=MESH).wait_recv()

    def local_value(c):
        return pltpu.make_async_copy(
            value_columns(me, c), rows_of(kv["own"][c], 1, me), local_sem.at[c])

    own_routes = [
        (has(4), "own", "Zm", frame + 4),
        (has(-4), "own", "Zp", frame - 4),
        (always, "own", "X", partner),
        (always, "own", "S", sibling),
    ]
    after_z = []
    if 8 < frames:
        into = ("P8", "P8") if 16 >= frames else ("M8", "P8")
        after_z += [
            (has(-4) & has(4), "Zm", into[0], frame + 4),
            (has(-4) & has(4), "Zp", into[1], frame - 4),
        ]
    after_z += [
        (low & has(4), "Zp", "ZX", partner),
        (high & has(-4), "Zm", "ZX", partner),
        (even_core & has(4), "Zp", "ZS", sibling),
        (odd_core & has(-4), "Zm", "ZS", sibling),
    ]
    after_x = [(always, "X", "XS", sibling)]
    after_zx = [(there["ZX"], "ZX", "ZXS", sibling)]
    after_power = []
    power = 8
    while power * 2 < frames:
        last = power * 4 >= frames
        after_power.append((power, [
            (has(-power) & has(power), "M%d" % power, ("P%d" if last else "M%d") % (2 * power), frame + power),
            (has(-power) & has(power), "P%d" % power, "P%d" % (2 * power), frame - power),
        ]))
        power = power * 2
    routes = own_routes + after_z + after_x + after_zx
    for _, extra in after_power:
        routes = routes + extra
    slot_of = {id(route): i for i, route in enumerate(routes)}

    def whole_copy(c, route):
        _, held, to, target = route
        return pltpu.make_async_remote_copy(
            src_ref=kv[held][c], dst_ref=kv[to][c], send_sem=seq_send.at[c, slot_of[id(route)]],
            recv_sem=seq_recv.at[c, where_of[to]], device_id=(target, me), device_id_type=MESH)

    def send(c, some):
        for route in some:
            @pl.when(route[0])
            def _(route=route):
                whole_copy(c, route).start()

    def send_part(c, which, group, src=None):
        for route in own_routes:
            @pl.when(route[0])
            def _(route=route):
                pltpu.make_async_remote_copy(
                    src_ref=rows_of(kv["own"][c], which, group) if src is None else src,
                    dst_ref=rows_of(kv[route[2]][c], which, group),
                    send_sem=seq_send.at[c, slot_of[id(route)]],
                    recv_sem=seq_recv.at[c, where_of[route[2]]],
                    device_id=(route[3], me), device_id_type=MESH).start()

    def wait_for(c, name):
        @pl.when(there[name])
        def _():
            pltpu.make_async_remote_copy(
                src_ref=kv[name][c], dst_ref=kv[name][c], send_sem=seq_send.at[c, 0],
                recv_sem=seq_recv.at[c, where_of[name]], device_id=(sibling, me),
                device_id_type=MESH).wait_recv()

    def turn_keys(c):
        for r in range(1, groups):
            turn(k_ref, staged(stage_k, r, c, True), column_of((me + r) % groups, c), c, True)
        turn(k_ref, rows_of(kv["own"][c], 0, me), column_of(me, c), c, True)

    def enter_queries(c):
        for r in range(1, groups):
            turn(q_ref, staged(stage_q, r, c, False), column_of((me + r) % groups, c), c, False)
            in_copy(c, r, 2).start()
        turn(q_ref, q_all[c].at[my_rows, :], column_of(me, c), c, False)

    two = ("S", "XS", "ZXS")
    early_names = ("S", "XS", "X", "Zm", "Zp", "ZS")
    late_names = [n for n in names if n not in early_names + ("own", "ZXS")] + ["ZXS"]

    def paired(some):
        slots = [(name, j) for name in some for j in range(2 if name in two else 1)]
        return [slots[i:i + 2] for i in range(0, len(slots), 2)]

    own_groups = [[("own", 2 * i), ("own", 2 * i + 1)] for i in range(tokens // (2 * BLK))]
    early, late = paired(early_names), paired(late_names)

    def attend(c, units, begin, finish, first, count):
        @pl.loop(0, count)
        def _(i):
            b = first + i
            at = pl.ds(pl.multiple_of(b * BLK, BLK), BLK)
            table_row = frame * frame_blocks + b
            start = {}
            bound = {}
            for name, j in [slot for unit in units for slot in unit if slot[0] != "own"]:
                source = jnp.clip(place[name], 0, frames - 1)
                block = kv_ref[table_row, source * SLOTS + j] - source * frame_blocks
                start[name, j] = jnp.clip(block, 0, frame_blocks - 1)
                usable = jnp.where(there[name], count_ref[source, table_row], 0) > j
                bound[name, j] = jnp.where(usable, jnp.float32(jnp.inf), jnp.float32(-jnp.inf))
            for h in range(sizes[c]):
                col = slice(h * HD, (h + 1) * HD)
                query = q_all[c][at, col]
                kept = begins[c] // HD + h - kept_from

                def side(unit, which):
                    name, j = unit[0]
                    if name == "own":
                        return kv[name][c][which, j:j + 2, :, col].reshape(2 * BLK, HD)
                    parts = [kv[name][c][which, start[name, j], :, col] for name, j in unit]
                    return jnp.concatenate(parts, axis=0) if len(parts) > 1 else parts[0]

                top = None if begin else tops[kept, b]
                for u, unit in enumerate(units):
                    s = lax.dot_general(query, side(unit, 0), (((1,), (1,)), ((), ())),
                                        preferred_element_type=jnp.float32)
                    for k, slot in enumerate(unit):
                        part = s[:, k * BLK:(k + 1) * BLK]
                        if slot[0] != "own":
                            part = jnp.minimum(part, bound[slot])
                        scores[h, u, :, k * BLK:(k + 1) * BLK] = part
                        top = part if top is None else jnp.maximum(top, part)
                top = jnp.max(top, axis=1, keepdims=True)
                if begin:
                    total = None
                    out = None
                else:
                    factor = jnp.exp2((tops[kept, b] - top) * EXP2_SCALE)
                    total = sums[kept, b] * factor
                    out = numerators[kept, b] * factor
                for u, unit in enumerate(units):
                    p = jnp.exp2((scores[h, u, :, :len(unit) * BLK] - top) * EXP2_SCALE)
                    for k in range(len(unit)):
                        part = p[:, k * BLK:(k + 1) * BLK]
                        total = part if total is None else total + part
                    term = jnp.dot(p.astype(jnp.bfloat16), side(unit, 1), preferred_element_type=jnp.float32)
                    out = term if out is None else out + term
                if finish:
                    total = jnp.sum(total, axis=1, keepdims=True)
                    att[c][at, col] = (out / total).astype(jnp.bfloat16)
                else:
                    tops[kept, b] = jnp.broadcast_to(top, (BLK, BLK))
                    sums[kept, b] = total
                    numerators[kept, b] = out

    def out_copy(c, r):
        target = (me + r) % groups
        at = pl.ds(pl.multiple_of(target * rows, rows), rows)
        return pltpu.make_async_remote_copy(
            src_ref=att[c].at[at, :], dst_ref=out_hbm.at[:, pl.ds(column_of(me, c), widths[c])],
            send_sem=out_send.at[c, r - 1], recv_sem=out_recv.at[c, r - 1],
            device_id=(frame, target), device_id_type=MESH)

    def out_block(c, r, i):
        target = (me + r) % groups
        at = pl.ds(pl.multiple_of(target * rows + i * BLK, BLK), BLK)
        return pltpu.make_async_remote_copy(
            src_ref=att[c].at[at, :],
            dst_ref=out_hbm.at[pl.ds(i * BLK, BLK), pl.ds(column_of(me, c), widths[c])],
            send_sem=out_send.at[c, r - 1], recv_sem=out_recv.at[c, r - 1],
            device_id=(frame, target), device_id_type=MESH)

    def out_wait(c, r):
        source = (me + groups - r) % groups
        at = out_hbm.at[:, pl.ds(column_of(source, c), widths[c])]
        pltpu.make_async_remote_copy(
            src_ref=at, dst_ref=at, send_sem=out_send.at[c, r - 1],
            recv_sem=out_recv.at[c, r - 1], device_id=(frame, source),
            device_id_type=MESH).wait_recv()

    def local_out(c):
        return pltpu.make_async_copy(
            att[c].at[my_rows, :], out_hbm.at[:, pl.ds(column_of(me, c), widths[c])], out_local.at[c])

    def leave(c):
        for r in range(1, groups):
            out_copy(c, r).start()
        local_out(c).start()

    def enter_values(c):
        send_part(c, 1, me, value_columns(me, c))
        for r in range(1, groups):
            in_copy(c, r, 1).start()

    def enter_keys(c):
        turn_keys(c)
        send_part(c, 0, me)
        for r in range(1, groups):
            in_copy(c, r, 0).start()

    pl.semaphore_wait(barrier, expected)
    ahead = min(2, chunks)
    for c in range(ahead):
        enter_values(c)
    load_turn.wait()
    load_k.wait()
    for c in range(chunks):
        enter_keys(c)
        if c + ahead < chunks:
            enter_values(c + ahead)
    for c in range(chunks):
        local_value(c).start()
    load_q.start()
    load_kv.start()
    load_count.start()
    load_q.wait()
    load_kv.wait()
    load_count.wait()
    for c in range(chunks):
        enter_queries(c)
    for name in names:
        if name in ("own", "S", "X", "XS"):
            continue

        @pl.when(jnp.logical_not(there[name]))
        def _(name=name):
            @pl.loop(0, frame_blocks)
            def _(i):
                for c in range(chunks):
                    for which in range(2):
                        kv[name][c][which, i] = jnp.zeros((BLK, widths[c]), jnp.bfloat16)

    for c in range(chunks):
        local_value(c).wait()
        for r in range(1, groups):
            for which in (1, 0):
                in_wait(c, r, which)
                send_part(c, which, (me + groups - r) % groups)
    for c in range(chunks):
        wait_for(c, "Zm")
        wait_for(c, "Zp")
        send(c, after_z)
        wait_for(c, "X")
        send(c, after_x)
    for c in range(one_pass, chunks):
        for name in ("S", "XS", "ZS"):
            wait_for(c, name)
        for r in range(1, groups):
            in_wait(c, r, 2)
        attend(c, own_groups + early, True, False, 0, frame_blocks)

    def drain_out(c):
        for r in range(1, groups):
            out_copy(c, r).wait_send()
            out_wait(c, r)
        local_out(c).wait()

    for c in range(chunks):
        wait_for(c, "ZX")
        send(c, after_zx)
        for power, some in after_power:
            wait_for(c, "M%d" % power)
            wait_for(c, "P%d" % power)
            send(c, some)
        if c == chunks - 1:
            for d in range(chunks):
                for r in range(1, groups):
                    for what in range(3):
                        in_copy(d, r, what).wait_send()
            for route in routes:
                @pl.when(route[0])
                def _(route=route):
                    for d in range(chunks - 1):
                        whole_copy(d, route).wait_send()
            for d in range(chunks - 2):
                drain_out(d)
        if len(names) > 9:
            wait_for(c, names[-1])
        for name in ("S", "XS", "ZS", "ZXS") if c < one_pass else ("ZXS",):
            wait_for(c, name)
        for r in range(1, groups):
            if c < one_pass:
                in_wait(c, r, 2)
        if c < one_pass:
            attend(c, own_groups + early + late, True, True, 0, frame_blocks)
            leave(c)
        elif whole_blocks:
            share = rows // BLK
            for r in range(1, groups):
                for i in range(share):
                    attend(c, late, False, True, (me + r) % groups * share + i, 1)
                    out_block(c, r, i).start()
            attend(c, late, False, True, me * share, share)
            local_out(c).start()
        else:
            attend(c, late, False, True, 0, frame_blocks)
            leave(c)

    for route in routes:
        @pl.when(route[0])
        def _(route=route):
            whole_copy(chunks - 1, route).wait_send()
    for c in range(max(chunks - 2, 0), chunks):
        drain_out(c)


def local(queries, keys, values, kv_blocks, block_counts):
    frames = lax.axis_size("seq")
    groups = lax.axis_size("head")
    rows, model = queries.shape
    heads = model // HD // groups
    sizes = chunk_sizes(heads)
    chunks = len(sizes)
    tokens = rows * groups
    names = source_names(frames)
    n_pairs = tokens // (2 * BLK) + (len(names) + 4) // 2
    plan = (frames, groups, rows, heads, sizes, tuple(names))
    n_routes = 10 + 2 * len(names)
    lead = (rows // BLK, BLK) if rows % BLK == 0 else (rows,)
    blocks = [pltpu.VMEM((2, tokens // BLK, BLK, size * HD), jnp.bfloat16) for size in sizes]
    flats = [pltpu.VMEM((tokens, size * HD), jnp.bfloat16) for size in sizes]
    group_width = heads * HD
    whole = pltpu.VMEM((rows, model), jnp.bfloat16)
    stage_q = pltpu.VMEM((max(groups - 1, 1), rows, group_width), jnp.bfloat16)
    stage_k = pltpu.VMEM((max(groups - 1, 1),) + lead + (group_width,), jnp.bfloat16)
    state = pltpu.VMEM((sum(sizes[-TWO_PASS:]), tokens // BLK, BLK, HD), jnp.float32)
    sem = pltpu.SemaphoreType.DMA
    others = max(groups - 1, 1)
    return pl.pallas_call(
        functools.partial(kernel, plan),
        out_shape=jax.ShapeDtypeStruct((rows, model), jnp.bfloat16),
        in_specs=[
            pl.BlockSpec(memory_space=pltpu.HBM),
            pl.BlockSpec(memory_space=pltpu.HBM),
            pl.BlockSpec(memory_space=pltpu.HBM),
            pl.BlockSpec(memory_space=pltpu.HBM),
            pl.BlockSpec(memory_space=pltpu.HBM),
            pl.BlockSpec(memory_space=pltpu.HBM),
        ],
        out_specs=pl.BlockSpec(memory_space=pltpu.VMEM),
        scratch_shapes=blocks * len(names) + flats * 2 + [
            pltpu.SMEM(kv_blocks.shape, jnp.int32),
            pltpu.SMEM(block_counts.shape[::-1], jnp.int32),
            pltpu.VMEM((8, HD), jnp.float32),
            whole,
            whole,
            stage_k,
            stage_q,
            pltpu.VMEM((max(sizes), n_pairs, BLK, 2 * BLK), jnp.float32),
            state,
            state,
            state,
            sem((chunks, others, 3)),
            sem((chunks, others, 3)),
            sem((chunks,)),
            sem((chunks, n_routes)),
            sem((chunks, len(names))),
            sem((chunks, others)),
            sem((chunks, others)),
            sem((chunks,)),
            sem((5,)),
        ],
        compiler_params=pltpu.CompilerParams(
            collective_id=0, has_side_effects=True, vmem_limit_bytes=50 * 1024 * 1024
        ),
    )(*[pltpu.with_memory_space_constraint(x, pltpu.HBM) for x in (
        kv_blocks, block_counts.T, jnp.asarray(turn_table(frames)), queries, keys,
        values.reshape(lead + (model,)))])


def solution(mesh):
    in_specs = (
        P(("seq", "head"), None),
        P(("seq", "head"), None),
        P(("seq", "head"), None),
        P(),
        P(),
    )
    out_specs = P(("seq", "head"), None)
    return jax.shard_map(local, mesh=mesh, in_specs=in_specs, out_specs=out_specs, check_vma=False)
```

```python
import functools
import math

import jax
import jax.numpy as jnp
import numpy as np
from jax import lax
from jax.experimental import pallas as pl
from jax.experimental.pallas import tpu as pltpu
from jax.sharding import PartitionSpec as P

HD = 128
BLK = 128
SLOTS = 4
TWO_PASS = 3
RESULTS = ("E", "X", "8m", "8p")
MESH = pl.DeviceIdType.MESH
EXP2_SCALE = HD ** (-0.5) * math.log2(math.e)


def turn_table(frames):
    lane = np.arange(HD)
    frequency = (256.0 ** (-(lane // 2) / 8.0)).astype(np.float32)
    angle = np.arange(frames, dtype=np.float32)[:, None] * frequency[None, :]
    cosine = np.cos(angle.astype(np.float64))
    sine = np.sin(angle.astype(np.float64))
    turned = lane < 16
    even = lane % 2 == 0
    table = np.zeros((frames, 8, HD), np.float32)
    table[:, 0] = np.where(turned, cosine, 1.0)
    table[:, 1] = np.where(turned & even, -sine, 0.0)
    table[:, 2] = np.where(turned & ~even, sine, 0.0)
    return table


def chunk_sizes(heads):
    if heads < 6:
        return (1,) * heads
    middle = heads - 6
    rest = (middle % 3,) if middle % 3 else ()
    return (1, 2) + (3,) * (middle // 3) + rest + (1, 1, 1)


def swaps(frames, groups, rows, sizes):
    return frames == 16 and groups == 2 and rows % BLK == 0 and len(sizes) > TWO_PASS and sizes[-1] == 1


def source_names(frames):
    names = ["own", "S", "X", "XS", "Zm", "Zp", "ZS", "ZX", "ZXS"]
    power = 8
    while power < frames:
        names += ["P%d" % power] if power * 2 >= frames else ["M%d" % power, "P%d" % power]
        power = power * 2
    return names


def kernel(plan, kv_hbm, count_hbm, turn_hbm, q_hbm, k_hbm, v_hbm, out_hbm, *scratch):
    frames, groups, rows, heads, sizes, names = plan
    chunks = len(sizes)
    one_pass = max(chunks - TWO_PASS, 0)
    swap = swaps(frames, groups, rows, sizes)
    last = chunks - 1
    ends = last if swap else chunks
    kept_from = sum(sizes[:one_pass])
    group_width = heads * HD
    widths = [size * HD for size in sizes]
    begins = [sum(widths[:c]) for c in range(chunks)]
    tokens = rows * groups
    frame_blocks = tokens // BLK
    scratch = list(scratch)

    def take(n):
        head, scratch[:] = scratch[:n], scratch[n:]
        return head

    kv = {name: take(chunks) for name in names}
    q_all = take(chunks)
    att = take(chunks)
    kv_ref, count_ref, turn_ref = take(3)
    q_ref, k_ref, stage_k, stage_q, scores, tops, sums, numerators = take(8)
    in_send, in_recv, local_sem, seq_send, seq_recv, out_send, out_recv, out_local, load_sem = take(9)
    where_of = {name: i for i, name in enumerate(names)}
    if swap:
        q_x, q_8m, q_8p, z_mine, z_theirs, from_x, from_8, from_x_log, from_8_log = take(9)
        part, part_log = dict(zip(RESULTS, take(4))), dict(zip(RESULTS, take(4)))
        other, other_log = dict(zip(RESULTS, take(4))), dict(zip(RESULTS, take(4)))
        swap_send, swap_recv = take(2)

    frame = lax.axis_index("seq")
    me = lax.axis_index("head")
    core = frame % 2
    parity = (frame // 2) % 2
    sibling = frame + 1 - 2 * core
    partner = frame + 2 - 4 * parity
    my_rows = pl.ds(pl.multiple_of(me * rows, rows), rows)
    whole_blocks = rows % BLK == 0
    always = frame >= 0
    even_core, odd_core = core == 0, core == 1
    low, high = parity == 0, parity == 1

    def has(o):
        return frame + o < frames if o > 0 else frame + o >= 0

    side_core = jnp.where(even_core, -4, 4)
    side_pair = jnp.where(low, -4, 4)
    place = {
        "own": frame,
        "S": sibling,
        "X": partner,
        "XS": sibling + partner - frame,
        "Zm": frame - 4,
        "Zp": frame + 4,
        "ZS": sibling + side_core,
        "ZX": partner + side_pair,
        "ZXS": sibling + partner - frame + side_pair,
    }
    for name in names[9:]:
        power = int(name[1:])
        if power * 2 >= frames:
            place[name] = frame + jnp.where(frame >= power, -power, power)
        else:
            place[name] = frame - power if name[0] == "M" else frame + power
    there = {name: (place[name] >= 0) & (place[name] < frames) for name in names}

    def rows_of(buffer, which, group):
        if whole_blocks:
            return buffer.at[which, pl.ds(group * (rows // BLK), rows // BLK)]
        first = group * rows
        return buffer.at[which, first // BLK, pl.ds(pl.multiple_of(first % BLK, rows), rows), :]

    steps = [4]
    while steps[-1] * 4 < frames:
        steps.append(steps[-1] * 2)

    load_k = pltpu.make_async_copy(k_hbm, k_ref, load_sem.at[0])
    load_q = pltpu.make_async_copy(q_hbm, q_ref, load_sem.at[1])
    load_turn = pltpu.make_async_copy(turn_hbm.at[frame], turn_ref, load_sem.at[2])
    load_kv = pltpu.make_async_copy(kv_hbm, kv_ref, load_sem.at[3])
    load_count = pltpu.make_async_copy(count_hbm, count_ref, load_sem.at[4])

    barrier = pltpu.get_barrier_semaphore()

    def greet(seq, head):
        pl.semaphore_signal(barrier, inc=1, device_id=(seq, head), device_id_type=MESH)

    expected = 2 + groups - 1
    for s in steps:
        for o in (-s, s):
            @pl.when(has(o))
            def _(o=o):
                greet(frame + o, me)

            expected = expected + jnp.where(has(o), 1, 0)
    greet(partner, me)
    for r in range(1, groups):
        greet(frame, (me + r) % groups)
    greet(sibling, me)
    load_turn.start()
    load_k.start()

    def turn(src, dst, column, c, blocked):
        cosine, up, down = turn_ref[0:1, :], turn_ref[1:2, :], turn_ref[2:3, :]
        piece = min(rows, 32)

        @pl.loop(0, rows // piece)
        def _(i):
            at = pl.ds(pl.multiple_of(i * piece, piece), piece)
            for h in range(sizes[c]):
                col = pl.ds(pl.multiple_of(column + h * HD, HD), HD)
                x = src[at, col].astype(jnp.float32)
                y = x * cosine + pltpu.roll(x, HD - 1, 1) * up + pltpu.roll(x, 1, 1) * down
                y = y.astype(jnp.bfloat16)
                lanes = slice(h * HD, (h + 1) * HD)
                if blocked and whole_blocks:
                    inner = pl.ds(pl.multiple_of(i * piece % BLK, piece), piece)
                    dst[i * piece // BLK, inner, lanes] = y
                else:
                    dst[at, lanes] = y

    def column_of(group, c):
        return pl.multiple_of(group * group_width + begins[c], HD)

    def staged(buffer, r, c, blocked):
        col = pl.ds(begins[c], widths[c])
        return buffer.at[r - 1, :, :, col] if blocked and whole_blocks else buffer.at[r - 1, :, col]

    def value_columns(group, c):
        col = pl.ds(column_of(group, c), widths[c])
        return v_hbm.at[:, :, col] if whole_blocks else v_hbm.at[:, col]

    def in_copy(c, r, what):
        target = (me + r) % groups
        if what == 0:
            src = staged(stage_k, r, c, True)
        elif what == 1:
            src = value_columns(target, c)
        else:
            src = staged(stage_q, r, c, False)
        dst = q_all[c].at[my_rows, :] if what == 2 else rows_of(kv["own"][c], what, me)
        return pltpu.make_async_remote_copy(
            src_ref=src, dst_ref=dst, send_sem=in_send.at[c, r - 1, what],
            recv_sem=in_recv.at[c, r - 1, what], device_id=(frame, target), device_id_type=MESH)

    def in_wait(c, r, what):
        source = (me + groups - r) % groups
        at = pl.ds(pl.multiple_of(source * rows, rows), rows)
        dst = q_all[c].at[at, :] if what == 2 else rows_of(kv["own"][c], what, source)
        pltpu.make_async_remote_copy(
            src_ref=dst, dst_ref=dst, send_sem=in_send.at[c, r - 1, what],
            recv_sem=in_recv.at[c, r - 1, what], device_id=(frame, source),
            device_id_type=MESH).wait_recv()

    def local_value(c):
        return pltpu.make_async_copy(
            value_columns(me, c), rows_of(kv["own"][c], 1, me), local_sem.at[c])

    own_routes = [
        (has(4), "own", "Zm", frame + 4),
        (has(-4), "own", "Zp", frame - 4),
        (always, "own", "X", partner),
        (always, "own", "S", sibling),
    ]
    after_z = []
    if 8 < frames:
        into = ("P8", "P8") if 16 >= frames else ("M8", "P8")
        after_z += [
            (has(-4) & has(4), "Zm", into[0], frame + 4),
            (has(-4) & has(4), "Zp", into[1], frame - 4),
        ]
    after_z += [
        (low & has(4), "Zp", "ZX", partner),
        (high & has(-4), "Zm", "ZX", partner),
        (even_core & has(4), "Zp", "ZS", sibling),
        (odd_core & has(-4), "Zm", "ZS", sibling),
    ]
    after_x = [(always, "X", "XS", sibling)]
    after_zx = [(there["ZX"], "ZX", "ZXS", sibling)]
    after_power = []
    power = 8
    while power * 2 < frames:
        last = power * 4 >= frames
        after_power.append((power, [
            (has(-power) & has(power), "M%d" % power, ("P%d" if last else "M%d") % (2 * power), frame + power),
            (has(-power) & has(power), "P%d" % power, "P%d" % (2 * power), frame - power),
        ]))
        power = power * 2
    routes = own_routes + after_z + after_x + after_zx
    for _, extra in after_power:
        routes = routes + extra
    slot_of = {id(route): i for i, route in enumerate(routes)}
    swapped = ("X", "XS", "ZX", "ZXS", "P8")

    def used(c, some):
        return [route for route in some if not (swap and c == last and route[2] in swapped)]

    def whole_copy(c, route):
        _, held, to, target = route
        return pltpu.make_async_remote_copy(
            src_ref=kv[held][c], dst_ref=kv[to][c], send_sem=seq_send.at[c, slot_of[id(route)]],
            recv_sem=seq_recv.at[c, where_of[to]], device_id=(target, me), device_id_type=MESH)

    def send(c, some):
        for route in used(c, some):
            @pl.when(route[0])
            def _(route=route):
                whole_copy(c, route).start()

    def send_part(c, which, group, src=None):
        for route in used(c, own_routes):
            @pl.when(route[0])
            def _(route=route):
                pltpu.make_async_remote_copy(
                    src_ref=rows_of(kv["own"][c], which, group) if src is None else src,
                    dst_ref=rows_of(kv[route[2]][c], which, group),
                    send_sem=seq_send.at[c, slot_of[id(route)]],
                    recv_sem=seq_recv.at[c, where_of[route[2]]],
                    device_id=(route[3], me), device_id_type=MESH).start()

    def wait_for(c, name):
        @pl.when(there[name])
        def _():
            pltpu.make_async_remote_copy(
                src_ref=kv[name][c], dst_ref=kv[name][c], send_sem=seq_send.at[c, 0],
                recv_sem=seq_recv.at[c, where_of[name]], device_id=(sibling, me),
                device_id_type=MESH).wait_recv()

    def turn_keys(c):
        for r in range(1, groups):
            turn(k_ref, staged(stage_k, r, c, True), column_of((me + r) % groups, c), c, True)
        turn(k_ref, rows_of(kv["own"][c], 0, me), column_of(me, c), c, True)

    def enter_queries(c):
        for r in range(1, groups):
            turn(q_ref, staged(stage_q, r, c, False), column_of((me + r) % groups, c), c, False)
            in_copy(c, r, 2).start()
        turn(q_ref, q_all[c].at[my_rows, :], column_of(me, c), c, False)

    two = ("S", "XS", "ZXS")
    early_names = ("S", "XS", "X", "Zm", "Zp", "ZS")
    late_names = [n for n in names if n not in early_names + ("own", "ZXS")] + ["ZXS"]

    def paired(some):
        slots = [(name, j) for name in some for j in range(2 if name in two else 1)]
        return [slots[i:i + 2] for i in range(0, len(slots), 2)]

    own_groups = [[("own", 2 * i), ("own", 2 * i + 1)] for i in range(tokens // (2 * BLK))]
    early, late = paired(early_names), paired(late_names)

    def attend(c, units, begin, finish, first, count):
        @pl.loop(0, count)
        def _(i):
            b = first + i
            at = pl.ds(pl.multiple_of(b * BLK, BLK), BLK)
            table_row = frame * frame_blocks + b
            start = {}
            bound = {}
            for name, j in [slot for unit in units for slot in unit if slot[0] != "own"]:
                source = jnp.clip(place[name], 0, frames - 1)
                block = kv_ref[table_row, source * SLOTS + j] - source * frame_blocks
                start[name, j] = jnp.clip(block, 0, frame_blocks - 1)
                usable = jnp.where(there[name], count_ref[source, table_row], 0) > j
                bound[name, j] = jnp.where(usable, jnp.float32(jnp.inf), jnp.float32(-jnp.inf))
            for h in range(sizes[c]):
                col = slice(h * HD, (h + 1) * HD)
                query = q_all[c][at, col]
                kept = begins[c] // HD + h - kept_from

                def side(unit, which):
                    name, j = unit[0]
                    if name == "own":
                        return kv[name][c][which, j:j + 2, :, col].reshape(2 * BLK, HD)
                    parts = [kv[name][c][which, start[name, j], :, col] for name, j in unit]
                    return jnp.concatenate(parts, axis=0) if len(parts) > 1 else parts[0]

                top = None if begin else tops[kept, b]
                for u, unit in enumerate(units):
                    s = lax.dot_general(query, side(unit, 0), (((1,), (1,)), ((), ())),
                                        preferred_element_type=jnp.float32)
                    for k, slot in enumerate(unit):
                        part = s[:, k * BLK:(k + 1) * BLK]
                        if slot[0] != "own":
                            part = jnp.minimum(part, bound[slot])
                        scores[h, u, :, k * BLK:(k + 1) * BLK] = part
                        top = part if top is None else jnp.maximum(top, part)
                top = jnp.max(top, axis=1, keepdims=True)
                if begin:
                    total = None
                    out = None
                else:
                    factor = jnp.exp2((tops[kept, b] - top) * EXP2_SCALE)
                    total = sums[kept, b] * factor
                    out = numerators[kept, b] * factor
                for u, unit in enumerate(units):
                    p = jnp.exp2((scores[h, u, :, :len(unit) * BLK] - top) * EXP2_SCALE)
                    for k in range(len(unit)):
                        part = p[:, k * BLK:(k + 1) * BLK]
                        total = part if total is None else total + part
                    term = jnp.dot(p.astype(jnp.bfloat16), side(unit, 1), preferred_element_type=jnp.float32)
                    out = term if out is None else out + term
                if finish:
                    total = jnp.sum(total, axis=1, keepdims=True)
                    att[c][at, col] = (out / total).astype(jnp.bfloat16)
                else:
                    tops[kept, b] = jnp.broadcast_to(top, (BLK, BLK))
                    sums[kept, b] = total
                    numerators[kept, b] = out

    def fold(query, units, table_row):
        start, bound = {}, {}
        for u, unit in enumerate(units):
            for k, (buffer, source, exists, j) in enumerate(unit):
                if source is None:
                    continue
                clipped = jnp.clip(source, 0, frames - 1)
                block = kv_ref[table_row, clipped * SLOTS + j] - clipped * frame_blocks
                start[u, k] = jnp.clip(block, 0, frame_blocks - 1)
                usable = jnp.where(exists, count_ref[clipped, table_row], 0) > j
                bound[u, k] = jnp.where(usable, jnp.float32(jnp.inf), jnp.float32(-jnp.inf))

        def side(u, which):
            parts = [buffer[which, j if source is None else start[u, k]]
                     for k, (buffer, source, exists, j) in enumerate(units[u])]
            return jnp.concatenate(parts, axis=0) if len(parts) > 1 else parts[0]

        top = None
        for u, unit in enumerate(units):
            s = lax.dot_general(query, side(u, 0), (((1,), (1,)), ((), ())), preferred_element_type=jnp.float32)
            for k, slot in enumerate(unit):
                piece = s[:, k * BLK:(k + 1) * BLK]
                if slot[1] is not None:
                    piece = jnp.minimum(piece, bound[u, k])
                scores[0, u, :, k * BLK:(k + 1) * BLK] = piece
                top = piece if top is None else jnp.maximum(top, piece)
        top = jnp.maximum(jnp.max(top, axis=1, keepdims=True), -1e30)
        total, out = None, None
        for u, unit in enumerate(units):
            p = jnp.exp2((scores[0, u, :, :len(unit) * BLK] - top) * EXP2_SCALE)
            for k in range(len(unit)):
                piece = p[:, k * BLK:(k + 1) * BLK]
                total = piece if total is None else total + piece
            term = jnp.dot(p.astype(jnp.bfloat16), side(u, 1), preferred_element_type=jnp.float32)
            out = term if out is None else out + term
        return top, jnp.sum(total, axis=1, keepdims=True), out

    def diagonal():
        return (lax.broadcasted_iota(jnp.int32, (BLK, BLK), 0) == lax.broadcasted_iota(jnp.int32, (BLK, BLK), 1))

    share = max(rows // BLK, 1)

    def partial(name, queries, query_frame, units):
        @pl.loop(0, frame_blocks)
        def _(b):
            query = queries[pl.ds(pl.multiple_of(b * BLK, BLK), BLK), :]
            top, total, out = fold(query, units, query_frame * frame_blocks + b)
            some = total > 0
            total = jnp.where(some, total, 1.0)
            log = jnp.where(some, top * EXP2_SCALE + jnp.log(total) * math.log2(math.e), -1e30)
            flat = jnp.sum(jnp.where(diagonal(), jnp.broadcast_to(log, (BLK, BLK)), 0.0), axis=0, keepdims=True)
            inner = b % share
            part[name][b // share, pl.ds(pl.multiple_of(inner * BLK, BLK), BLK), :] = (out / total).astype(jnp.bfloat16)
            part_log[name][b // share, inner] = jnp.broadcast_to(flat, (8, BLK))

    def remote(src, dst, send, recv, seq, head):
        return pltpu.make_async_remote_copy(
            src_ref=src, dst_ref=dst, send_sem=swap_send.at[send], recv_sem=swap_recv.at[recv],
            device_id=(seq, head), device_id_type=MESH)

    middle = (frame >= 4) & (frame < 12)
    first_half = frame < 8
    over = frame + jnp.where(first_half, 4, -4)
    peer = (me + 1) % groups
    exists_of = {"E": always, "X": always, "8m": middle, "8p": middle}

    def queries_out(what):
        if what == 0:
            return always, remote(q_all[last], q_x, 0, 0, partner, me)
        if what == 1:
            return first_half, remote(q_all[last], q_8m, 1, 1, over, me)
        return jnp.logical_not(first_half), remote(q_all[last], q_8p, 2, 2, over, me)

    def sibling_keys():
        return remote(z_mine, z_theirs, 3, 3, sibling, me)

    def mine(source):
        return pltpu.make_async_copy(source, z_mine, swap_send.at[4])

    def across(i, log):
        name = RESULTS[i]
        if log:
            return remote(part_log[name].at[peer], other_log[name], 9 + i, 9 + i, frame, peer)
        return remote(part[name].at[peer], other[name], 5 + i, 5 + i, frame, peer)

    def returns(name):
        to, to_log = (from_x, from_x_log) if name == "X" else (from_8, from_8_log)
        send = {"X": 13, "8m": 15, "8p": 17}[name]
        recv = 13 if name == "X" else 15
        target = {"X": partner, "8m": frame - 4, "8p": frame + 4}[name]
        return [
            remote(part[name].at[me], to.at[me], send, recv, target, me),
            remote(other[name], to.at[peer], send, recv, target, me),
            remote(part_log[name].at[me], to_log.at[me], send + 1, recv + 1, target, me),
            remote(other_log[name], to_log.at[peer], send + 1, recv + 1, target, me),
        ]

    def returned(name, to, to_log):
        send = {"X": 13, "8m": 15, "8p": 17}[name]
        recv = 13 if name == "X" else 15
        return [remote(to, to, send, recv, partner, me), remote(to_log, to_log, send + 1, recv + 1, partner, me)]

    def swap_queries():
        for r in range(1, groups):
            in_wait(last, r, 2)
        for what in range(3):
            condition, copy = queries_out(what)

            @pl.when(condition)
            def _(copy=copy):
                copy.start()

    def swap_keys():
        for source, condition in (("Zm", high), ("Zp", low)):
            @pl.when(condition)
            def _(source=source):
                mine(kv[source][last]).start()
                mine(kv[source][last]).wait()
        sibling_keys().start()

    def swap_partials():
        own, near, minus, plus = (kv[name][last] for name in ("own", "S", "Zm", "Zp"))
        for name in ("S", "ZS"):
            wait_for(last, name)

        @pl.when(middle)
        def _():
            remote(q_8m, q_8m, 1, 1, sibling, me).wait_recv()
            partial("8m", q_8m, frame - 4, [[(plus, frame + 4, middle, 0)]])
            remote(q_8p, q_8p, 2, 2, sibling, me).wait_recv()
            partial("8p", q_8p, frame + 4, [[(minus, frame - 4, middle, 0)]])
            for i in (2, 3):
                across(i, False).start()
                across(i, True).start()

        remote(q_x, q_x, 0, 0, sibling, me).wait_recv()
        sibling_keys().wait_recv()
        far = frame - side_pair
        far_there = (far >= 0) & (far < frames)
        sibling_far = sibling - side_pair
        partial("X", q_x, partner, [
            [(near, sibling, always, 0), (near, sibling, always, 1)],
            [(own, frame, always, 0), (z_mine, far, far_there, 0)],
            [(z_theirs, sibling_far, far_there, 0), (z_theirs, sibling_far, far_there, 1)],
        ])
        across(1, False).start()
        across(1, True).start()
        partial("E", q_all[last], frame, [
            [(own, None, None, 2 * i + k) for k in range(2)] for i in range(frame_blocks // 2)
        ] + [
            [(near, sibling, always, 0), (near, sibling, always, 1)],
            [(minus, place["Zm"], there["Zm"], 0), (plus, place["Zp"], there["Zp"], 0)],
            [(kv["ZS"][last], place["ZS"], there["ZS"], 0)],
        ])
        across(0, False).start()
        across(0, True).start()

    def swap_returns():
        for i in (2, 3, 1):
            name = RESULTS[i]

            @pl.when(exists_of[name])
            def _(i=i, name=name):
                across(i, False).wait_recv()
                across(i, True).wait_recv()
                for copy in returns(name):
                    copy.start()

    def swap_merge():
        across(0, False).wait_recv()
        across(0, True).wait_recv()
        for copy in returned("X", from_x, from_x_log) + returned("8m", from_8, from_8_log):
            copy.wait_recv()
        for group, early_part, early_log in ((me, part["E"].at[me], part_log["E"].at[me]), (peer, other["E"], other_log["E"])):
            col = pl.ds(column_of(group, last), HD)
            for i in range(share):
                at = slice(i * BLK, (i + 1) * BLK)
                logs = [early_log[i, 0:1], from_x_log[group, i, 0:1], from_8_log[group, i, 0:1]]
                numbers = [early_part[at, :], from_x[group, at, :], from_8[group, at, :]]
                top = jnp.maximum(jnp.maximum(logs[0], logs[1]), logs[2])
                weights = [jnp.exp2(log - top) for log in logs]
                total = weights[0] + weights[1] + weights[2]
                out = None
                for weight, number in zip(weights, numbers):
                    flat = jnp.broadcast_to(weight / total, (BLK, BLK))
                    column = jnp.sum(jnp.where(diagonal(), flat, 0.0), axis=1, keepdims=True)
                    term = column * number.astype(jnp.float32)
                    out = term if out is None else out + term
                out_hbm[at, col] = out.astype(jnp.bfloat16)

    def swap_drain():
        for what in range(3):
            condition, copy = queries_out(what)

            @pl.when(condition)
            def _(copy=copy):
                copy.wait_send()
        sibling_keys().wait_send()
        for i, name in enumerate(RESULTS):
            @pl.when(exists_of[name])
            def _(i=i, name=name):
                across(i, False).wait_send()
                across(i, True).wait_send()
                if name != "E":
                    for copy in returned(name, from_x if name == "X" else from_8, from_x_log if name == "X" else from_8_log):
                        copy.wait_send()

    def out_copy(c, r):
        target = (me + r) % groups
        at = pl.ds(pl.multiple_of(target * rows, rows), rows)
        return pltpu.make_async_remote_copy(
            src_ref=att[c].at[at, :], dst_ref=out_hbm.at[:, pl.ds(column_of(me, c), widths[c])],
            send_sem=out_send.at[c, r - 1], recv_sem=out_recv.at[c, r - 1],
            device_id=(frame, target), device_id_type=MESH)

    def out_block(c, r, i):
        target = (me + r) % groups
        at = pl.ds(pl.multiple_of(target * rows + i * BLK, BLK), BLK)
        return pltpu.make_async_remote_copy(
            src_ref=att[c].at[at, :],
            dst_ref=out_hbm.at[pl.ds(i * BLK, BLK), pl.ds(column_of(me, c), widths[c])],
            send_sem=out_send.at[c, r - 1], recv_sem=out_recv.at[c, r - 1],
            device_id=(frame, target), device_id_type=MESH)

    def out_wait(c, r):
        source = (me + groups - r) % groups
        at = out_hbm.at[:, pl.ds(column_of(source, c), widths[c])]
        pltpu.make_async_remote_copy(
            src_ref=at, dst_ref=at, send_sem=out_send.at[c, r - 1],
            recv_sem=out_recv.at[c, r - 1], device_id=(frame, source),
            device_id_type=MESH).wait_recv()

    def local_out(c):
        return pltpu.make_async_copy(
            att[c].at[my_rows, :], out_hbm.at[:, pl.ds(column_of(me, c), widths[c])], out_local.at[c])

    def leave(c):
        for r in range(1, groups):
            out_copy(c, r).start()
        local_out(c).start()

    def enter_values(c):
        send_part(c, 1, me, value_columns(me, c))
        for r in range(1, groups):
            in_copy(c, r, 1).start()

    def enter_keys(c):
        turn_keys(c)
        send_part(c, 0, me)
        for r in range(1, groups):
            in_copy(c, r, 0).start()

    pl.semaphore_wait(barrier, expected)
    ahead = min(2, chunks)
    for c in range(ahead):
        enter_values(c)
    load_turn.wait()
    load_k.wait()
    for c in range(chunks):
        enter_keys(c)
        if c + ahead < chunks:
            enter_values(c + ahead)
    for c in range(chunks):
        local_value(c).start()
    load_q.start()
    load_kv.start()
    load_count.start()
    load_q.wait()
    load_kv.wait()
    load_count.wait()
    for c in ([last] if swap else []) + list(range(ends)):
        enter_queries(c)
    for name in names:
        if name in ("own", "S", "X", "XS"):
            continue

        @pl.when(jnp.logical_not(there[name]))
        def _(name=name):
            @pl.loop(0, frame_blocks)
            def _(i):
                for c in range(chunks):
                    for which in range(2):
                        kv[name][c][which, i] = jnp.zeros((BLK, widths[c]), jnp.bfloat16)

    for c in range(chunks):
        local_value(c).wait()
        for r in range(1, groups):
            for which in (1, 0):
                in_wait(c, r, which)
                send_part(c, which, (me + groups - r) % groups)
    if swap:
        swap_queries()
    for c in range(chunks):
        wait_for(c, "Zm")
        wait_for(c, "Zp")
        send(c, after_z)
        if c < ends:
            wait_for(c, "X")
            send(c, after_x)
        else:
            swap_keys()
    if swap:
        swap_partials()
    for c in range(one_pass, ends):
        for name in ("S", "XS", "ZS"):
            wait_for(c, name)
        for r in range(1, groups):
            in_wait(c, r, 2)
        attend(c, own_groups + early, True, False, 0, frame_blocks)

    if swap:
        swap_returns()

    def drain_out(c):
        for r in range(1, groups):
            out_copy(c, r).wait_send()
            out_wait(c, r)
        local_out(c).wait()

    for c in range(ends):
        wait_for(c, "ZX")
        send(c, after_zx)
        for power, some in after_power:
            wait_for(c, "M%d" % power)
            wait_for(c, "P%d" % power)
            send(c, some)
        if c == ends - 1:
            for d in range(chunks):
                for r in range(1, groups):
                    for what in range(3):
                        in_copy(d, r, what).wait_send()
            for route in routes:
                @pl.when(route[0])
                def _(route=route):
                    for d in range(ends - 1):
                        whole_copy(d, route).wait_send()
            for d in range(ends - 2):
                drain_out(d)
        if len(names) > 9:
            wait_for(c, names[-1])
        for name in ("S", "XS", "ZS", "ZXS") if c < one_pass else ("ZXS",):
            wait_for(c, name)
        for r in range(1, groups):
            if c < one_pass:
                in_wait(c, r, 2)
        if c < one_pass:
            attend(c, own_groups + early + late, True, True, 0, frame_blocks)
            leave(c)
        elif whole_blocks:
            share = rows // BLK
            for r in range(1, groups):
                for i in range(share):
                    attend(c, late, False, True, (me + r) % groups * share + i, 1)
                    out_block(c, r, i).start()
            attend(c, late, False, True, me * share, share)
            local_out(c).start()
        else:
            attend(c, late, False, True, 0, frame_blocks)
            leave(c)

    for route in routes:
        @pl.when(route[0])
        def _(route=route):
            for c in range(ends - 1, chunks):
                if used(c, [route]):
                    whole_copy(c, route).wait_send()
    for c in range(max(ends - 2, 0), ends):
        drain_out(c)
    if swap:
        swap_drain()
        swap_merge()


def local(queries, keys, values, kv_blocks, block_counts):
    frames = lax.axis_size("seq")
    groups = lax.axis_size("head")
    rows, model = queries.shape
    heads = model // HD // groups
    sizes = chunk_sizes(heads)
    chunks = len(sizes)
    tokens = rows * groups
    names = source_names(frames)
    n_pairs = tokens // (2 * BLK) + (len(names) + 4) // 2
    plan = (frames, groups, rows, heads, sizes, tuple(names))
    n_routes = 10 + 2 * len(names)
    lead = (rows // BLK, BLK) if rows % BLK == 0 else (rows,)
    blocks = [pltpu.VMEM((2, tokens // BLK, BLK, size * HD), jnp.bfloat16) for size in sizes]
    flats = [pltpu.VMEM((tokens, size * HD), jnp.bfloat16) for size in sizes]
    group_width = heads * HD
    whole = pltpu.VMEM((rows, model), jnp.bfloat16)
    stage_q = pltpu.VMEM((max(groups - 1, 1), rows, group_width), jnp.bfloat16)
    stage_k = pltpu.VMEM((max(groups - 1, 1),) + lead + (group_width,), jnp.bfloat16)
    state = pltpu.VMEM((sum(sizes[-TWO_PASS:]), tokens // BLK, BLK, HD), jnp.float32)
    sem = pltpu.SemaphoreType.DMA
    others = max(groups - 1, 1)
    swap_scratch = []
    if swaps(frames, groups, rows, sizes):
        half = pltpu.VMEM((rows, HD), jnp.bfloat16)
        halves = pltpu.VMEM((groups, rows, HD), jnp.bfloat16)
        log = pltpu.VMEM((rows // BLK, 8, BLK), jnp.float32)
        logs = pltpu.VMEM((groups, rows // BLK, 8, BLK), jnp.float32)
        swap_scratch = [pltpu.VMEM((tokens, HD), jnp.bfloat16)] * 3 + [blocks[-1]] * 2 + [halves, halves, logs, logs]
        swap_scratch += [halves] * 4 + [logs] * 4 + [half] * 4 + [log] * 4 + [sem((20,)), sem((20,))]
    return pl.pallas_call(
        functools.partial(kernel, plan),
        out_shape=jax.ShapeDtypeStruct((rows, model), jnp.bfloat16),
        in_specs=[
            pl.BlockSpec(memory_space=pltpu.HBM),
            pl.BlockSpec(memory_space=pltpu.HBM),
            pl.BlockSpec(memory_space=pltpu.HBM),
            pl.BlockSpec(memory_space=pltpu.HBM),
            pl.BlockSpec(memory_space=pltpu.HBM),
            pl.BlockSpec(memory_space=pltpu.HBM),
        ],
        out_specs=pl.BlockSpec(memory_space=pltpu.VMEM),
        scratch_shapes=blocks * len(names) + flats * 2 + [
            pltpu.SMEM(kv_blocks.shape, jnp.int32),
            pltpu.SMEM(block_counts.shape[::-1], jnp.int32),
            pltpu.VMEM((8, HD), jnp.float32),
            whole,
            whole,
            stage_k,
            stage_q,
            pltpu.VMEM((max(sizes), n_pairs, BLK, 2 * BLK), jnp.float32),
            state,
            state,
            state,
            sem((chunks, others, 3)),
            sem((chunks, others, 3)),
            sem((chunks,)),
            sem((chunks, n_routes)),
            sem((chunks, len(names))),
            sem((chunks, others)),
            sem((chunks, others)),
            sem((chunks,)),
            sem((5,)),
        ] + swap_scratch,
        compiler_params=pltpu.CompilerParams(
            collective_id=0, has_side_effects=True, vmem_limit_bytes=50 * 1024 * 1024
        ),
    )(*[pltpu.with_memory_space_constraint(x, pltpu.HBM) for x in (
        kv_blocks, block_counts.T, jnp.asarray(turn_table(frames)), queries, keys,
        values.reshape(lead + (model,)))])


def solution(mesh):
    in_specs = (
        P(("seq", "head"), None),
        P(("seq", "head"), None),
        P(("seq", "head"), None),
        P(),
        P(),
    )
    out_specs = P(("seq", "head"), None)
    return jax.shard_map(local, mesh=mesh, in_specs=in_specs, out_specs=out_specs, check_vma=False)
```

```python
import functools
import math

import jax
import jax.numpy as jnp
import numpy as np
from jax import lax
from jax.experimental import pallas as pl
from jax.experimental.pallas import tpu as pltpu
from jax.sharding import PartitionSpec as P

HD = 128
BLK = 128
SLOTS = 4
TWO_PASS = 3
RESULTS = ("E", "X", "8m", "8p")
MESH = pl.DeviceIdType.MESH
EXP2_SCALE = HD ** (-0.5) * math.log2(math.e)


def turn_table(frames):
    lane = np.arange(HD)
    frequency = (256.0 ** (-(lane // 2) / 8.0)).astype(np.float32)
    angle = np.arange(frames, dtype=np.float32)[:, None] * frequency[None, :]
    cosine = np.cos(angle.astype(np.float64))
    sine = np.sin(angle.astype(np.float64))
    turned = lane < 16
    even = lane % 2 == 0
    table = np.zeros((frames, 8, HD), np.float32)
    table[:, 0] = np.where(turned, cosine, 1.0)
    table[:, 1] = np.where(turned & even, -sine, 0.0)
    table[:, 2] = np.where(turned & ~even, sine, 0.0)
    return table


def chunk_sizes(heads):
    if heads < 6:
        return (1,) * heads
    middle = heads - 6
    rest = (middle % 3,) if middle % 3 else ()
    return (2,) + (3,) * (middle // 3) + rest + (2, 1, 1)


def swaps(frames, groups, rows, sizes):
    return (frames == 16 and groups == 2 and rows % BLK == 0 and rows <= 4 * BLK
            and len(sizes) > TWO_PASS and sizes[-1] == 1)


def source_names(frames):
    names = ["own", "S", "X", "XS", "Zm", "Zp", "ZS", "ZX", "ZXS"]
    power = 8
    while power < frames:
        names += ["P%d" % power] if power * 2 >= frames else ["M%d" % power, "P%d" % power]
        power = power * 2
    return names


def kernel(plan, kv_hbm, count_hbm, turn_hbm, q_hbm, k_hbm, v_hbm, out_hbm, *scratch):
    frames, groups, rows, heads, sizes, names = plan
    chunks = len(sizes)
    one_pass = max(chunks - TWO_PASS, 0)
    swap = swaps(frames, groups, rows, sizes)
    last = chunks - 1
    ends = last if swap else chunks
    kept_from = sum(sizes[:one_pass])
    group_width = heads * HD
    widths = [size * HD for size in sizes]
    begins = [sum(widths[:c]) for c in range(chunks)]
    tokens = rows * groups
    frame_blocks = tokens // BLK
    scratch = list(scratch)

    def take(n):
        head, scratch[:] = scratch[:n], scratch[n:]
        return head

    kv = {name: take(chunks) for name in names}
    q_all = take(chunks)
    att = take(chunks)
    kv_ref, count_ref, turn_ref = take(3)
    q_ref, k_ref, stage_k, stage_q, scores, tops, sums, numerators = take(8)
    in_send, in_recv, local_sem, seq_send, seq_recv, out_send, out_recv, out_local, load_sem = take(9)
    where_of = {name: i for i, name in enumerate(names)}
    if swap:
        q_x, q_8m, q_8p, z_mine, z_theirs, from_x, from_8, from_x_stat, from_8_stat = take(9)
        part, part_stat = dict(zip(RESULTS, take(4))), dict(zip(RESULTS, take(4)))
        other, other_stat = dict(zip(RESULTS, take(4))), dict(zip(RESULTS, take(4)))
        near, near_stat, swap_send, swap_recv = take(4)

    frame = lax.axis_index("seq")
    me = lax.axis_index("head")
    core = frame % 2
    parity = (frame // 2) % 2
    sibling = frame + 1 - 2 * core
    partner = frame + 2 - 4 * parity
    my_rows = pl.ds(pl.multiple_of(me * rows, rows), rows)
    whole_blocks = rows % BLK == 0
    always = frame >= 0
    even_core, odd_core = core == 0, core == 1
    low, high = parity == 0, parity == 1

    def has(o):
        return frame + o < frames if o > 0 else frame + o >= 0

    side_core = jnp.where(even_core, -4, 4)
    side_pair = jnp.where(low, -4, 4)
    place = {
        "own": frame,
        "S": sibling,
        "X": partner,
        "XS": sibling + partner - frame,
        "Zm": frame - 4,
        "Zp": frame + 4,
        "ZS": sibling + side_core,
        "ZX": partner + side_pair,
        "ZXS": sibling + partner - frame + side_pair,
    }
    for name in names[9:]:
        power = int(name[1:])
        if power * 2 >= frames:
            place[name] = frame + jnp.where(frame >= power, -power, power)
        else:
            place[name] = frame - power if name[0] == "M" else frame + power
    there = {name: (place[name] >= 0) & (place[name] < frames) for name in names}

    def rows_of(buffer, which, group):
        if whole_blocks:
            return buffer.at[which, pl.ds(group * (rows // BLK), rows // BLK)]
        first = group * rows
        return buffer.at[which, first // BLK, pl.ds(pl.multiple_of(first % BLK, rows), rows), :]

    steps = [4]
    while steps[-1] * 4 < frames:
        steps.append(steps[-1] * 2)

    load_k = pltpu.make_async_copy(k_hbm, k_ref, load_sem.at[0])
    load_q = pltpu.make_async_copy(q_hbm, q_ref, load_sem.at[1])
    load_turn = pltpu.make_async_copy(turn_hbm.at[frame], turn_ref, load_sem.at[2])
    load_kv = pltpu.make_async_copy(kv_hbm, kv_ref, load_sem.at[3])
    load_count = pltpu.make_async_copy(count_hbm, count_ref, load_sem.at[4])

    barrier = pltpu.get_barrier_semaphore()

    def greet(seq, head):
        pl.semaphore_signal(barrier, inc=1, device_id=(seq, head), device_id_type=MESH)

    expected = 2 + groups - 1
    for s in steps:
        for o in (-s, s):
            @pl.when(has(o))
            def _(o=o):
                greet(frame + o, me)

            expected = expected + jnp.where(has(o), 1, 0)
    greet(partner, me)
    for r in range(1, groups):
        greet(frame, (me + r) % groups)
    greet(sibling, me)
    load_turn.start()
    load_k.start()

    def turn(src, dst, column, c, blocked):
        cosine, up, down = turn_ref[0:1, :], turn_ref[1:2, :], turn_ref[2:3, :]
        piece = min(rows, 32)

        @pl.loop(0, rows // piece)
        def _(i):
            at = pl.ds(pl.multiple_of(i * piece, piece), piece)
            for h in range(sizes[c]):
                col = pl.ds(pl.multiple_of(column + h * HD, HD), HD)
                x = src[at, col].astype(jnp.float32)
                y = x * cosine + pltpu.roll(x, HD - 1, 1) * up + pltpu.roll(x, 1, 1) * down
                y = y.astype(jnp.bfloat16)
                lanes = slice(h * HD, (h + 1) * HD)
                if blocked and whole_blocks:
                    inner = pl.ds(pl.multiple_of(i * piece % BLK, piece), piece)
                    dst[i * piece // BLK, inner, lanes] = y
                else:
                    dst[at, lanes] = y

    def column_of(group, c):
        return pl.multiple_of(group * group_width + begins[c], HD)

    def staged(buffer, r, c, blocked):
        col = pl.ds(begins[c], widths[c])
        return buffer.at[r - 1, :, :, col] if blocked and whole_blocks else buffer.at[r - 1, :, col]

    def value_columns(group, c):
        col = pl.ds(column_of(group, c), widths[c])
        return v_hbm.at[:, :, col] if whole_blocks else v_hbm.at[:, col]

    def in_copy(c, r, what):
        target = (me + r) % groups
        if what == 0:
            src = staged(stage_k, r, c, True)
        elif what == 1:
            src = value_columns(target, c)
        else:
            src = staged(stage_q, r, c, False)
        dst = q_all[c].at[my_rows, :] if what == 2 else rows_of(kv["own"][c], what, me)
        return pltpu.make_async_remote_copy(
            src_ref=src, dst_ref=dst, send_sem=in_send.at[c, r - 1, what],
            recv_sem=in_recv.at[c, r - 1, what], device_id=(frame, target), device_id_type=MESH)

    def in_wait(c, r, what):
        source = (me + groups - r) % groups
        at = pl.ds(pl.multiple_of(source * rows, rows), rows)
        dst = q_all[c].at[at, :] if what == 2 else rows_of(kv["own"][c], what, source)
        pltpu.make_async_remote_copy(
            src_ref=dst, dst_ref=dst, send_sem=in_send.at[c, r - 1, what],
            recv_sem=in_recv.at[c, r - 1, what], device_id=(frame, source),
            device_id_type=MESH).wait_recv()

    def local_value(c):
        return pltpu.make_async_copy(
            value_columns(me, c), rows_of(kv["own"][c], 1, me), local_sem.at[c])

    own_routes = [
        (has(4), "own", "Zm", frame + 4),
        (has(-4), "own", "Zp", frame - 4),
        (always, "own", "X", partner),
        (always, "own", "S", sibling),
    ]
    after_z = []
    if 8 < frames:
        into = ("P8", "P8") if 16 >= frames else ("M8", "P8")
        after_z += [
            (has(-4) & has(4), "Zm", into[0], frame + 4),
            (has(-4) & has(4), "Zp", into[1], frame - 4),
        ]
    after_z += [
        (low & has(4), "Zp", "ZX", partner),
        (high & has(-4), "Zm", "ZX", partner),
        (even_core & has(4), "Zp", "ZS", sibling),
        (odd_core & has(-4), "Zm", "ZS", sibling),
    ]
    after_x = [(always, "X", "XS", sibling)]
    after_zx = [(there["ZX"], "ZX", "ZXS", sibling)]
    after_power = []
    power = 8
    while power * 2 < frames:
        last = power * 4 >= frames
        after_power.append((power, [
            (has(-power) & has(power), "M%d" % power, ("P%d" if last else "M%d") % (2 * power), frame + power),
            (has(-power) & has(power), "P%d" % power, "P%d" % (2 * power), frame - power),
        ]))
        power = power * 2
    routes = own_routes + after_z + after_x + after_zx
    for _, extra in after_power:
        routes = routes + extra
    slot_of = {id(route): i for i, route in enumerate(routes)}
    swapped = ("X", "XS", "ZX", "ZXS", "P8")

    def used(c, some):
        return [route for route in some if not (swap and c == last and route[2] in swapped)]

    def whole_copy(c, route):
        _, held, to, target = route
        return pltpu.make_async_remote_copy(
            src_ref=kv[held][c], dst_ref=kv[to][c], send_sem=seq_send.at[c, slot_of[id(route)]],
            recv_sem=seq_recv.at[c, where_of[to]], device_id=(target, me), device_id_type=MESH)

    def send(c, some):
        for route in used(c, some):
            @pl.when(route[0])
            def _(route=route):
                whole_copy(c, route).start()

    def send_part(c, which, group, src=None):
        for route in used(c, own_routes):
            @pl.when(route[0])
            def _(route=route):
                pltpu.make_async_remote_copy(
                    src_ref=rows_of(kv["own"][c], which, group) if src is None else src,
                    dst_ref=rows_of(kv[route[2]][c], which, group),
                    send_sem=seq_send.at[c, slot_of[id(route)]],
                    recv_sem=seq_recv.at[c, where_of[route[2]]],
                    device_id=(route[3], me), device_id_type=MESH).start()

    def both_of(buffer, group):
        if whole_blocks:
            return buffer.at[:, pl.ds(group * (rows // BLK), rows // BLK)]
        first = group * rows
        return buffer.at[:, first // BLK, pl.ds(pl.multiple_of(first % BLK, rows), rows), :]

    def send_both(c, group):
        for route in used(c, own_routes):
            @pl.when(route[0])
            def _(route=route):
                pltpu.make_async_remote_copy(
                    src_ref=both_of(kv["own"][c], group),
                    dst_ref=both_of(kv[route[2]][c], group),
                    send_sem=seq_send.at[c, slot_of[id(route)]],
                    recv_sem=seq_recv.at[c, where_of[route[2]]],
                    device_id=(route[3], me), device_id_type=MESH).start()

    def wait_for(c, name):
        @pl.when(there[name])
        def _():
            pltpu.make_async_remote_copy(
                src_ref=kv[name][c], dst_ref=kv[name][c], send_sem=seq_send.at[c, 0],
                recv_sem=seq_recv.at[c, where_of[name]], device_id=(sibling, me),
                device_id_type=MESH).wait_recv()

    def turn_keys(c):
        for r in range(1, groups):
            turn(k_ref, staged(stage_k, r, c, True), column_of((me + r) % groups, c), c, True)
        turn(k_ref, rows_of(kv["own"][c], 0, me), column_of(me, c), c, True)

    def enter_queries(c):
        for r in range(1, groups):
            turn(q_ref, staged(stage_q, r, c, False), column_of((me + r) % groups, c), c, False)
            in_copy(c, r, 2).start()
        turn(q_ref, q_all[c].at[my_rows, :], column_of(me, c), c, False)

    two = ("S", "XS", "ZXS")
    early_names = ("S", "XS", "X", "Zm", "Zp", "ZS")
    late_names = [n for n in names if n not in early_names + ("own", "ZXS")] + ["ZXS"]

    def paired(some):
        slots = [(name, j) for name in some for j in range(2 if name in two else 1)]
        return [slots[i:i + 2] for i in range(0, len(slots), 2)]

    own_groups = [[("own", 2 * i), ("own", 2 * i + 1)] for i in range(tokens // (2 * BLK))]
    early, late = paired(early_names), paired(late_names)

    def attend(c, units, begin, finish, first, count):
        @pl.loop(0, count)
        def _(i):
            b = first + i
            at = pl.ds(pl.multiple_of(b * BLK, BLK), BLK)
            table_row = frame * frame_blocks + b
            start = {}
            bound = {}
            for name, j in [slot for unit in units for slot in unit if slot[0] != "own"]:
                source = jnp.clip(place[name], 0, frames - 1)
                block = kv_ref[table_row, source * SLOTS + j] - source * frame_blocks
                start[name, j] = jnp.clip(block, 0, frame_blocks - 1)
                usable = jnp.where(there[name], count_ref[source, table_row], 0) > j
                bound[name, j] = jnp.where(usable, jnp.float32(jnp.inf), jnp.float32(-jnp.inf))
            for h in range(sizes[c]):
                col = slice(h * HD, (h + 1) * HD)
                query = q_all[c][at, col]
                kept = begins[c] // HD + h - kept_from

                def side(unit, which):
                    name, j = unit[0]
                    if name == "own":
                        return kv[name][c][which, j:j + 2, :, col].reshape(2 * BLK, HD)
                    parts = [kv[name][c][which, start[name, j], :, col] for name, j in unit]
                    return jnp.concatenate(parts, axis=0) if len(parts) > 1 else parts[0]

                top = None if begin else tops[kept, b]
                for u, unit in enumerate(units):
                    s = lax.dot_general(query, side(unit, 0), (((1,), (1,)), ((), ())),
                                        preferred_element_type=jnp.float32)
                    for k, slot in enumerate(unit):
                        part = s[:, k * BLK:(k + 1) * BLK]
                        if slot[0] != "own":
                            part = jnp.minimum(part, bound[slot])
                        scores[h, u, :, k * BLK:(k + 1) * BLK] = part
                        top = part if top is None else jnp.maximum(top, part)
                top = jnp.max(top, axis=1, keepdims=True)
                if begin:
                    total = None
                    out = None
                else:
                    factor = jnp.exp2((tops[kept, b] - top) * EXP2_SCALE)
                    total = sums[kept, b] * factor
                    out = numerators[kept, b] * factor
                for u, unit in enumerate(units):
                    p = jnp.exp2((scores[h, u, :, :len(unit) * BLK] - top) * EXP2_SCALE)
                    for k in range(len(unit)):
                        part = p[:, k * BLK:(k + 1) * BLK]
                        total = part if total is None else total + part
                    term = jnp.dot(p.astype(jnp.bfloat16), side(unit, 1), preferred_element_type=jnp.float32)
                    out = term if out is None else out + term
                if finish:
                    total = jnp.sum(total, axis=1, keepdims=True)
                    att[c][at, col] = (out / total).astype(jnp.bfloat16)
                else:
                    tops[kept, b] = jnp.broadcast_to(top, (BLK, BLK))
                    sums[kept, b] = total
                    numerators[kept, b] = out

    def fold(query, units, table_row):
        start, bound = {}, {}
        for u, unit in enumerate(units):
            for k, (buffer, source, exists, j) in enumerate(unit):
                if source is None:
                    continue
                clipped = jnp.clip(source, 0, frames - 1)
                block = kv_ref[table_row, clipped * SLOTS + j] - clipped * frame_blocks
                start[u, k] = jnp.clip(block, 0, frame_blocks - 1)
                usable = jnp.where(exists, count_ref[clipped, table_row], 0) > j
                bound[u, k] = jnp.where(usable, jnp.float32(jnp.inf), jnp.float32(-jnp.inf))

        def side(u, which):
            parts = [buffer[which, j if source is None else start[u, k]]
                     for k, (buffer, source, exists, j) in enumerate(units[u])]
            return jnp.concatenate(parts, axis=0) if len(parts) > 1 else parts[0]

        top = None
        for u, unit in enumerate(units):
            s = lax.dot_general(query, side(u, 0), (((1,), (1,)), ((), ())), preferred_element_type=jnp.float32)
            for k, slot in enumerate(unit):
                piece = s[:, k * BLK:(k + 1) * BLK]
                if slot[1] is not None:
                    piece = jnp.minimum(piece, bound[u, k])
                scores[0, u, :, k * BLK:(k + 1) * BLK] = piece
                top = piece if top is None else jnp.maximum(top, piece)
        top = jnp.maximum(jnp.max(top, axis=1, keepdims=True), -1e30)
        total, out = None, None
        for u, unit in enumerate(units):
            p = jnp.exp2((scores[0, u, :, :len(unit) * BLK] - top) * EXP2_SCALE)
            for k in range(len(unit)):
                piece = p[:, k * BLK:(k + 1) * BLK]
                total = piece if total is None else total + piece
            term = jnp.dot(p.astype(jnp.bfloat16), side(u, 1), preferred_element_type=jnp.float32)
            out = term if out is None else out + term
        return top, jnp.sum(total, axis=1, keepdims=True), out

    def diagonal():
        return (lax.broadcasted_iota(jnp.int32, (BLK, BLK), 0) == lax.broadcasted_iota(jnp.int32, (BLK, BLK), 1))

    share = max(rows // BLK, 1)

    def partial(name, queries, query_frame, units):
        @pl.loop(0, frame_blocks)
        def _(b):
            query = queries[pl.ds(pl.multiple_of(b * BLK, BLK), BLK), :]
            top, total, out = fold(query, units, query_frame * frame_blocks + b)
            inner = b % share
            half = b // share
            number = out / jnp.where(total > 0, total, 1.0)
            part[name][half, pl.ds(pl.multiple_of(inner * BLK, BLK), BLK), :] = number.astype(jnp.bfloat16)
            for k, column in enumerate((top, total)):
                flat = jnp.where(diagonal(), jnp.broadcast_to(column, (BLK, BLK)), 0.0)
                part_stat[name][half, pl.ds(4 * k + inner, 1), :] = jnp.sum(flat, axis=0, keepdims=True)

    def remote(src, dst, send, recv, seq, head):
        return pltpu.make_async_remote_copy(
            src_ref=src, dst_ref=dst, send_sem=swap_send.at[send], recv_sem=swap_recv.at[recv],
            device_id=(seq, head), device_id_type=MESH)

    middle = (frame >= 4) & (frame < 12)
    first_half = frame < 8
    over = frame + jnp.where(first_half, 4, -4)
    peer = (me + 1) % groups
    exists_of = {"E": always, "X": always, "8m": middle, "8p": middle}

    def queries_out(what):
        if what == 0:
            return always, remote(q_all[last], q_x, 0, 0, partner, me)
        if what == 1:
            return first_half, remote(q_all[last], q_8m, 1, 1, over, me)
        return jnp.logical_not(first_half), remote(q_all[last], q_8p, 2, 2, over, me)

    def sibling_keys():
        return remote(z_mine, z_theirs, 3, 3, sibling, me)

    def mine(source):
        return pltpu.make_async_copy(source, z_mine, swap_send.at[4])

    def across(i, stat):
        name = RESULTS[i]
        if stat:
            return remote(part_stat[name].at[peer], other_stat[name], 9 + i, 9 + i, frame, peer)
        return remote(part[name].at[peer], other[name], 5 + i, 5 + i, frame, peer)

    def returns(name):
        to, to_stat = (from_x, from_x_stat) if name == "X" else (from_8, from_8_stat)
        send = {"X": 13, "8m": 15, "8p": 17}[name]
        recv = 13 if name == "X" else 15
        target = {"X": partner, "8m": frame - 4, "8p": frame + 4}[name]
        return [
            remote(part_stat[name].at[me], to_stat.at[me], send + 1, recv + 1, target, me),
            remote(other_stat[name], to_stat.at[peer], send + 1, recv + 1, target, me),
            remote(part[name].at[me], to.at[me], send, recv, target, me),
            remote(other[name], to.at[peer], send, recv, target, me),
        ]

    def returned(name, to, to_stat):
        send = {"X": 13, "8m": 15, "8p": 17}[name]
        recv = 13 if name == "X" else 15
        return [remote(to, to, send, recv, partner, me), remote(to_stat, to_stat, send + 1, recv + 1, partner, me)]

    def swap_queries():
        for r in range(1, groups):
            in_wait(last, r, 2)
        for what in range(3):
            condition, copy = queries_out(what)

            @pl.when(condition)
            def _(copy=copy):
                copy.start()

    def swap_keys():
        for source, condition in (("Zm", high), ("Zp", low)):
            @pl.when(condition)
            def _(source=source):
                mine(kv[source][last]).start()
                mine(kv[source][last]).wait()
        sibling_keys().start()

    def swap_partials():
        own, beside, minus, plus = (kv[name][last] for name in ("own", "S", "Zm", "Zp"))
        for name in ("S", "ZS"):
            wait_for(last, name)

        @pl.when(middle)
        def _():
            remote(q_8m, q_8m, 1, 1, sibling, me).wait_recv()
            partial("8m", q_8m, frame - 4, [[(plus, frame + 4, middle, 0)]])
            remote(q_8p, q_8p, 2, 2, sibling, me).wait_recv()
            partial("8p", q_8p, frame + 4, [[(minus, frame - 4, middle, 0)]])
            for i in (2, 3):
                across(i, False).start()
                across(i, True).start()

        remote(q_x, q_x, 0, 0, sibling, me).wait_recv()
        sibling_keys().wait_recv()
        far = frame - side_pair
        far_there = (far >= 0) & (far < frames)
        sibling_far = sibling - side_pair
        partial("X", q_x, partner, [
            [(beside, sibling, always, 0), (beside, sibling, always, 1)],
            [(own, frame, always, 0), (z_mine, far, far_there, 0)],
            [(z_theirs, sibling_far, far_there, 0), (z_theirs, sibling_far, far_there, 1)],
        ])
        across(1, False).start()
        across(1, True).start()
        partial("E", q_all[last], frame, [
            [(own, None, None, 2 * i + k) for k in range(2)] for i in range(frame_blocks // 2)
        ] + [
            [(beside, sibling, always, 0), (beside, sibling, always, 1)],
            [(minus, place["Zm"], there["Zm"], 0), (plus, place["Zp"], there["Zp"], 0)],
            [(kv["ZS"][last], place["ZS"], there["ZS"], 0)],
        ])
        across(0, False).start()
        across(0, True).start()

    def swap_returns():
        for i in (2, 3, 1):
            name = RESULTS[i]

            @pl.when(exists_of[name])
            def _(i=i, name=name):
                across(i, False).wait_recv()
                across(i, True).wait_recv()
                for copy in returns(name):
                    copy.start()

    def column_from(flat):
        return jnp.sum(jnp.where(diagonal(), jnp.broadcast_to(flat, (BLK, BLK)), 0.0), axis=1, keepdims=True)

    def joined(stat_a, stat_b, i):
        top_a, top_b = stat_a[i:i + 1], stat_b[i:i + 1]
        top = jnp.maximum(top_a, top_b)
        weight_a = stat_a[4 + i:5 + i] * jnp.exp2((top_a - top) * EXP2_SCALE)
        weight_b = stat_b[4 + i:5 + i] * jnp.exp2((top_b - top) * EXP2_SCALE)
        total = weight_a + weight_b
        return top, total, weight_b / total

    def swap_near():
        across(0, False).wait_recv()
        across(0, True).wait_recv()
        for copy in returned("X", from_x, from_x_stat):
            copy.wait_recv()
        for g, group in enumerate((me, peer)):
            early_part, early_stat = (part["E"], part_stat["E"][me]) if g == 0 else (other["E"], other_stat["E"][...])
            x_stat = from_x_stat[group]
            for i in range(share):
                at = slice(i * BLK, (i + 1) * BLK)
                top, total, weight = joined(early_stat, x_stat, i)
                near_stat[g, i:i + 1, :] = top
                near_stat[g, 4 + i:5 + i, :] = total
                number = (early_part[me, at, :] if g == 0 else early_part[at, :]).astype(jnp.float32)
                near[g, at, :] = number + column_from(weight) * (from_x[group, at, :].astype(jnp.float32) - number)

    def swap_merge():
        for copy in returned("8m", from_8, from_8_stat):
            copy.wait_recv()
        for g, group in enumerate((me, peer)):
            col = pl.ds(column_of(group, last), HD)
            stat, stat_8 = near_stat[g], from_8_stat[group]
            for i in range(share):
                at = slice(i * BLK, (i + 1) * BLK)
                _, _, weight = joined(stat, stat_8, i)
                number = near[g, at, :]
                number = number + column_from(weight) * (from_8[group, at, :].astype(jnp.float32) - number)
                out_hbm[at, col] = number.astype(jnp.bfloat16)

    def swap_drain():
        for what in range(3):
            condition, copy = queries_out(what)

            @pl.when(condition)
            def _(copy=copy):
                copy.wait_send()
        sibling_keys().wait_send()
        for i, name in enumerate(RESULTS):
            @pl.when(exists_of[name])
            def _(i=i, name=name):
                across(i, False).wait_send()
                across(i, True).wait_send()
                if name != "E":
                    for copy in returned(name, from_x if name == "X" else from_8, from_x_stat if name == "X" else from_8_stat):
                        copy.wait_send()

    def out_copy(c, r):
        target = (me + r) % groups
        at = pl.ds(pl.multiple_of(target * rows, rows), rows)
        return pltpu.make_async_remote_copy(
            src_ref=att[c].at[at, :], dst_ref=out_hbm.at[:, pl.ds(column_of(me, c), widths[c])],
            send_sem=out_send.at[c, r - 1], recv_sem=out_recv.at[c, r - 1],
            device_id=(frame, target), device_id_type=MESH)

    def out_block(c, r, i):
        target = (me + r) % groups
        at = pl.ds(pl.multiple_of(target * rows + i * BLK, BLK), BLK)
        return pltpu.make_async_remote_copy(
            src_ref=att[c].at[at, :],
            dst_ref=out_hbm.at[pl.ds(i * BLK, BLK), pl.ds(column_of(me, c), widths[c])],
            send_sem=out_send.at[c, r - 1], recv_sem=out_recv.at[c, r - 1],
            device_id=(frame, target), device_id_type=MESH)

    def out_wait(c, r):
        source = (me + groups - r) % groups
        at = out_hbm.at[:, pl.ds(column_of(source, c), widths[c])]
        pltpu.make_async_remote_copy(
            src_ref=at, dst_ref=at, send_sem=out_send.at[c, r - 1],
            recv_sem=out_recv.at[c, r - 1], device_id=(frame, source),
            device_id_type=MESH).wait_recv()

    def local_out(c):
        return pltpu.make_async_copy(
            att[c].at[my_rows, :], out_hbm.at[:, pl.ds(column_of(me, c), widths[c])], out_local.at[c])

    def leave(c):
        for r in range(1, groups):
            out_copy(c, r).start()
        local_out(c).start()

    def enter_values(c):
        send_part(c, 1, me, value_columns(me, c))
        for r in range(1, groups):
            in_copy(c, r, 1).start()

    def enter_keys(c):
        turn_keys(c)
        send_part(c, 0, me)
        for r in range(1, groups):
            in_copy(c, r, 0).start()

    pl.semaphore_wait(barrier, expected)
    ahead = min(2, chunks)
    for c in range(ahead):
        enter_values(c)
    load_turn.wait()
    load_k.wait()
    for c in range(chunks):
        enter_keys(c)
        if c + ahead < chunks:
            enter_values(c + ahead)
    for c in range(chunks):
        local_value(c).start()
    load_q.start()
    load_kv.start()
    load_count.start()
    load_q.wait()
    load_kv.wait()
    load_count.wait()
    for c in ([last] if swap else []) + list(range(ends)):
        enter_queries(c)
    for name in names:
        if name in ("own", "S", "X", "XS"):
            continue

        @pl.when(jnp.logical_not(there[name]))
        def _(name=name):
            @pl.loop(0, frame_blocks)
            def _(i):
                for c in range(chunks):
                    for which in range(2):
                        kv[name][c][which, i] = jnp.zeros((BLK, widths[c]), jnp.bfloat16)

    for c in range(chunks):
        local_value(c).wait()
        for r in range(1, groups):
            for which in (1, 0):
                in_wait(c, r, which)
            send_both(c, (me + groups - r) % groups)
    if swap:
        swap_queries()
    for c in range(chunks):
        wait_for(c, "Zm")
        wait_for(c, "Zp")
        send(c, after_z)
        if c < ends:
            wait_for(c, "X")
            send(c, after_x)
        else:
            swap_keys()
    if swap:
        swap_partials()
    for c in range(one_pass, ends):
        for name in ("S", "XS", "ZS"):
            wait_for(c, name)
        for r in range(1, groups):
            in_wait(c, r, 2)
        attend(c, own_groups + early, True, False, 0, frame_blocks)

    if swap:
        swap_returns()

    def drain_out(c):
        for r in range(1, groups):
            out_copy(c, r).wait_send()
            out_wait(c, r)
        local_out(c).wait()

    for c in range(ends):
        wait_for(c, "ZX")
        send(c, after_zx)
        for power, some in after_power:
            wait_for(c, "M%d" % power)
            wait_for(c, "P%d" % power)
            send(c, some)
        if c == ends - 1:
            for d in range(chunks):
                for r in range(1, groups):
                    for what in range(3):
                        in_copy(d, r, what).wait_send()
            for route in routes:
                @pl.when(route[0])
                def _(route=route):
                    for d in range(ends - 1):
                        whole_copy(d, route).wait_send()
            for d in range(ends - 2):
                drain_out(d)
        if len(names) > 9:
            wait_for(c, names[-1])
        for name in ("S", "XS", "ZS", "ZXS") if c < one_pass else ("ZXS",):
            wait_for(c, name)
        for r in range(1, groups):
            if c < one_pass:
                in_wait(c, r, 2)
        if c < one_pass:
            attend(c, own_groups + early + late, True, True, 0, frame_blocks)
            leave(c)
        elif whole_blocks:
            share = rows // BLK
            for r in range(1, groups):
                for i in range(share):
                    attend(c, late, False, True, (me + r) % groups * share + i, 1)
                    out_block(c, r, i).start()
            attend(c, late, False, True, me * share, share)
            local_out(c).start()
        else:
            attend(c, late, False, True, 0, frame_blocks)
            leave(c)

    for route in routes:
        @pl.when(route[0])
        def _(route=route):
            for c in range(ends - 1, chunks):
                if used(c, [route]):
                    whole_copy(c, route).wait_send()
    for c in range(max(ends - 2, 0), ends):
        drain_out(c)
    if swap:
        swap_near()
        swap_drain()
        swap_merge()


def local(queries, keys, values, kv_blocks, block_counts):
    frames = lax.axis_size("seq")
    groups = lax.axis_size("head")
    rows, model = queries.shape
    heads = model // HD // groups
    sizes = chunk_sizes(heads)
    chunks = len(sizes)
    tokens = rows * groups
    names = source_names(frames)
    n_pairs = tokens // (2 * BLK) + (len(names) + 4) // 2
    plan = (frames, groups, rows, heads, sizes, tuple(names))
    n_routes = 10 + 2 * len(names)
    lead = (rows // BLK, BLK) if rows % BLK == 0 else (rows,)
    blocks = [pltpu.VMEM((2, tokens // BLK, BLK, size * HD), jnp.bfloat16) for size in sizes]
    flats = [pltpu.VMEM((tokens, size * HD), jnp.bfloat16) for size in sizes]
    group_width = heads * HD
    whole = pltpu.VMEM((rows, model), jnp.bfloat16)
    stage_q = pltpu.VMEM((max(groups - 1, 1), rows, group_width), jnp.bfloat16)
    stage_k = pltpu.VMEM((max(groups - 1, 1),) + lead + (group_width,), jnp.bfloat16)
    state = pltpu.VMEM((sum(sizes[-TWO_PASS:]), tokens // BLK, BLK, HD), jnp.float32)
    sem = pltpu.SemaphoreType.DMA
    others = max(groups - 1, 1)
    swap_scratch = []
    if swaps(frames, groups, rows, sizes):
        half = pltpu.VMEM((rows, HD), jnp.bfloat16)
        halves = pltpu.VMEM((groups, rows, HD), jnp.bfloat16)
        stat = pltpu.VMEM((8, BLK), jnp.float32)
        stats = pltpu.VMEM((groups, 8, BLK), jnp.float32)
        swap_scratch = [pltpu.VMEM((tokens, HD), jnp.bfloat16)] * 3 + [blocks[-1]] * 2 + [halves, halves, stats, stats]
        swap_scratch += [halves] * 4 + [stats] * 4 + [half] * 4 + [stat] * 4
        swap_scratch += [pltpu.VMEM((groups, rows, HD), jnp.float32), stats, sem((20,)), sem((20,))]
    return pl.pallas_call(
        functools.partial(kernel, plan),
        out_shape=jax.ShapeDtypeStruct((rows, model), jnp.bfloat16),
        in_specs=[
            pl.BlockSpec(memory_space=pltpu.HBM),
            pl.BlockSpec(memory_space=pltpu.HBM),
            pl.BlockSpec(memory_space=pltpu.HBM),
            pl.BlockSpec(memory_space=pltpu.HBM),
            pl.BlockSpec(memory_space=pltpu.HBM),
            pl.BlockSpec(memory_space=pltpu.HBM),
        ],
        out_specs=pl.BlockSpec(memory_space=pltpu.VMEM),
        scratch_shapes=blocks * len(names) + flats * 2 + [
            pltpu.SMEM(kv_blocks.shape, jnp.int32),
            pltpu.SMEM(block_counts.shape[::-1], jnp.int32),
            pltpu.VMEM((8, HD), jnp.float32),
            whole,
            whole,
            stage_k,
            stage_q,
            pltpu.VMEM((max(sizes), n_pairs, BLK, 2 * BLK), jnp.float32),
            state,
            state,
            state,
            sem((chunks, others, 3)),
            sem((chunks, others, 3)),
            sem((chunks,)),
            sem((chunks, n_routes)),
            sem((chunks, len(names))),
            sem((chunks, others)),
            sem((chunks, others)),
            sem((chunks,)),
            sem((5,)),
        ] + swap_scratch,
        compiler_params=pltpu.CompilerParams(
            collective_id=0, has_side_effects=True, vmem_limit_bytes=50 * 1024 * 1024
        ),
    )(*[pltpu.with_memory_space_constraint(x, pltpu.HBM) for x in (
        kv_blocks, block_counts.T, jnp.asarray(turn_table(frames)), queries, keys,
        values.reshape(lead + (model,)))])


def solution(mesh):
    in_specs = (
        P(("seq", "head"), None),
        P(("seq", "head"), None),
        P(("seq", "head"), None),
        P(),
        P(),
    )
    out_specs = P(("seq", "head"), None)
    return jax.shard_map(local, mesh=mesh, in_specs=in_specs, out_specs=out_specs, check_vma=False)
```

```python
import functools
import math

import jax
import jax.numpy as jnp
import numpy as np
from jax import lax
from jax.experimental import pallas as pl
from jax.experimental.pallas import tpu as pltpu
from jax.sharding import PartitionSpec as P

HD = 128
BLK = 128
SLOTS = 4
TWO_PASS = 4
RESULTS = ("E", "X", "8m", "8p")
MESH = pl.DeviceIdType.MESH
EXP2_SCALE = HD ** (-0.5) * math.log2(math.e)


def turn_table(frames):
    lane = np.arange(HD)
    frequency = (256.0 ** (-(lane // 2) / 8.0)).astype(np.float32)
    angle = np.arange(frames, dtype=np.float32)[:, None] * frequency[None, :]
    cosine = np.cos(angle.astype(np.float64))
    sine = np.sin(angle.astype(np.float64))
    turned = lane < 16
    even = lane % 2 == 0
    table = np.zeros((frames, 8, HD), np.float32)
    table[:, 0] = np.where(turned, cosine, 1.0)
    table[:, 1] = np.where(turned & even, -sine, 0.0)
    table[:, 2] = np.where(turned & ~even, sine, 0.0)
    return table


def chunk_sizes(heads):
    if heads < 6:
        return (1,) * heads
    middle = heads - 6
    rest = (middle % 3,) if middle % 3 else ()
    return (2,) + (3,) * (middle // 3) + rest + (2, 1, 1)


def swaps(frames, groups, rows, sizes):
    return (frames == 16 and groups == 2 and rows % BLK == 0 and rows <= 4 * BLK
            and len(sizes) > TWO_PASS and sizes[-1] == 1)


def source_names(frames):
    names = ["own", "S", "X", "XS", "Zm", "Zp", "ZS", "ZX", "ZXS"]
    power = 8
    while power < frames:
        names += ["P%d" % power] if power * 2 >= frames else ["M%d" % power, "P%d" % power]
        power = power * 2
    return names


def kernel(plan, kv_hbm, count_hbm, turn_hbm, q_hbm, k_hbm, v_hbm, out_hbm, *scratch):
    frames, groups, rows, heads, sizes, names = plan
    chunks = len(sizes)
    one_pass = max(chunks - TWO_PASS, 0)
    swap = swaps(frames, groups, rows, sizes)
    last = chunks - 1
    ends = last if swap else chunks
    kept_from = sum(sizes[:one_pass])
    group_width = heads * HD
    widths = [size * HD for size in sizes]
    begins = [sum(widths[:c]) for c in range(chunks)]
    tokens = rows * groups
    frame_blocks = tokens // BLK
    scratch = list(scratch)

    def take(n):
        head, scratch[:] = scratch[:n], scratch[n:]
        return head

    kv = {name: take(chunks) for name in names}
    q_all = take(chunks)
    att = take(chunks)
    kv_ref, count_ref, turn_ref = take(3)
    q_ref, k_ref, stage_k, stage_q, scores, tops, sums, numerators = take(8)
    in_send, in_recv, local_sem, seq_send, seq_recv, out_send, out_recv, out_local, load_sem = take(9)
    where_of = {name: i for i, name in enumerate(names)}
    if swap:
        q_x, q_8m, q_8p, z_mine, z_theirs, from_x, from_8, from_x_stat, from_8_stat = take(9)
        part, part_stat = dict(zip(RESULTS, take(4))), dict(zip(RESULTS, take(4)))
        other, other_stat = dict(zip(RESULTS, take(4))), dict(zip(RESULTS, take(4)))
        near, near_stat, swap_send, swap_recv = take(4)

    frame = lax.axis_index("seq")
    me = lax.axis_index("head")
    core = frame % 2
    parity = (frame // 2) % 2
    sibling = frame + 1 - 2 * core
    partner = frame + 2 - 4 * parity
    my_rows = pl.ds(pl.multiple_of(me * rows, rows), rows)
    whole_blocks = rows % BLK == 0
    always = frame >= 0
    even_core, odd_core = core == 0, core == 1
    low, high = parity == 0, parity == 1

    def has(o):
        return frame + o < frames if o > 0 else frame + o >= 0

    side_core = jnp.where(even_core, -4, 4)
    side_pair = jnp.where(low, -4, 4)
    place = {
        "own": frame,
        "S": sibling,
        "X": partner,
        "XS": sibling + partner - frame,
        "Zm": frame - 4,
        "Zp": frame + 4,
        "ZS": sibling + side_core,
        "ZX": partner + side_pair,
        "ZXS": sibling + partner - frame + side_pair,
    }
    for name in names[9:]:
        power = int(name[1:])
        if power * 2 >= frames:
            place[name] = frame + jnp.where(frame >= power, -power, power)
        else:
            place[name] = frame - power if name[0] == "M" else frame + power
    there = {name: (place[name] >= 0) & (place[name] < frames) for name in names}

    def rows_of(buffer, which, group):
        if whole_blocks:
            return buffer.at[which, pl.ds(group * (rows // BLK), rows // BLK)]
        first = group * rows
        return buffer.at[which, first // BLK, pl.ds(pl.multiple_of(first % BLK, rows), rows), :]

    steps = [4]
    while steps[-1] * 4 < frames:
        steps.append(steps[-1] * 2)

    load_k = pltpu.make_async_copy(k_hbm, k_ref, load_sem.at[0])
    load_q = pltpu.make_async_copy(q_hbm, q_ref, load_sem.at[1])
    load_turn = pltpu.make_async_copy(turn_hbm.at[frame], turn_ref, load_sem.at[2])
    load_kv = pltpu.make_async_copy(kv_hbm, kv_ref, load_sem.at[3])
    load_count = pltpu.make_async_copy(count_hbm, count_ref, load_sem.at[4])

    barrier = pltpu.get_barrier_semaphore()

    def greet(seq, head):
        pl.semaphore_signal(barrier, inc=1, device_id=(seq, head), device_id_type=MESH)

    expected = 2 + groups - 1
    for s in steps:
        for o in (-s, s):
            @pl.when(has(o))
            def _(o=o):
                greet(frame + o, me)

            expected = expected + jnp.where(has(o), 1, 0)
    greet(partner, me)
    for r in range(1, groups):
        greet(frame, (me + r) % groups)
    greet(sibling, me)
    load_turn.start()
    load_k.start()

    def turn(src, dst, column, c, blocked):
        cosine, up, down = turn_ref[0:1, :], turn_ref[1:2, :], turn_ref[2:3, :]
        piece = min(rows, 32)

        @pl.loop(0, rows // piece)
        def _(i):
            at = pl.ds(pl.multiple_of(i * piece, piece), piece)
            for h in range(sizes[c]):
                col = pl.ds(pl.multiple_of(column + h * HD, HD), HD)
                x = src[at, col].astype(jnp.float32)
                y = x * cosine + pltpu.roll(x, HD - 1, 1) * up + pltpu.roll(x, 1, 1) * down
                y = y.astype(jnp.bfloat16)
                lanes = slice(h * HD, (h + 1) * HD)
                if blocked and whole_blocks:
                    inner = pl.ds(pl.multiple_of(i * piece % BLK, piece), piece)
                    dst[i * piece // BLK, inner, lanes] = y
                else:
                    dst[at, lanes] = y

    def column_of(group, c):
        return pl.multiple_of(group * group_width + begins[c], HD)

    def staged(buffer, r, c, blocked):
        col = pl.ds(begins[c], widths[c])
        return buffer.at[r - 1, :, :, col] if blocked and whole_blocks else buffer.at[r - 1, :, col]

    def value_columns(group, c):
        col = pl.ds(column_of(group, c), widths[c])
        return v_hbm.at[:, :, col] if whole_blocks else v_hbm.at[:, col]

    def in_copy(c, r, what):
        target = (me + r) % groups
        if what == 0:
            src = staged(stage_k, r, c, True)
        elif what == 1:
            src = value_columns(target, c)
        else:
            src = staged(stage_q, r, c, False)
        dst = q_all[c].at[my_rows, :] if what == 2 else rows_of(kv["own"][c], what, me)
        return pltpu.make_async_remote_copy(
            src_ref=src, dst_ref=dst, send_sem=in_send.at[c, r - 1, what],
            recv_sem=in_recv.at[c, r - 1, what], device_id=(frame, target), device_id_type=MESH)

    def in_wait(c, r, what):
        source = (me + groups - r) % groups
        at = pl.ds(pl.multiple_of(source * rows, rows), rows)
        dst = q_all[c].at[at, :] if what == 2 else rows_of(kv["own"][c], what, source)
        pltpu.make_async_remote_copy(
            src_ref=dst, dst_ref=dst, send_sem=in_send.at[c, r - 1, what],
            recv_sem=in_recv.at[c, r - 1, what], device_id=(frame, source),
            device_id_type=MESH).wait_recv()

    def local_value(c):
        return pltpu.make_async_copy(
            value_columns(me, c), rows_of(kv["own"][c], 1, me), local_sem.at[c])

    own_routes = [
        (has(4), "own", "Zm", frame + 4),
        (has(-4), "own", "Zp", frame - 4),
        (always, "own", "X", partner),
        (always, "own", "S", sibling),
    ]
    after_z = []
    if 8 < frames:
        into = ("P8", "P8") if 16 >= frames else ("M8", "P8")
        after_z += [
            (has(-4) & has(4), "Zm", into[0], frame + 4),
            (has(-4) & has(4), "Zp", into[1], frame - 4),
        ]
    after_z += [
        (low & has(4), "Zp", "ZX", partner),
        (high & has(-4), "Zm", "ZX", partner),
        (even_core & has(4), "Zp", "ZS", sibling),
        (odd_core & has(-4), "Zm", "ZS", sibling),
    ]
    after_x = [(always, "X", "XS", sibling)]
    after_zx = [(there["ZX"], "ZX", "ZXS", sibling)]
    after_power = []
    power = 8
    while power * 2 < frames:
        last = power * 4 >= frames
        after_power.append((power, [
            (has(-power) & has(power), "M%d" % power, ("P%d" if last else "M%d") % (2 * power), frame + power),
            (has(-power) & has(power), "P%d" % power, "P%d" % (2 * power), frame - power),
        ]))
        power = power * 2
    routes = own_routes + after_z + after_x + after_zx
    for _, extra in after_power:
        routes = routes + extra
    slot_of = {id(route): i for i, route in enumerate(routes)}
    swapped = ("X", "XS", "ZX", "ZXS", "P8")

    def used(c, some):
        return [route for route in some if not (swap and c == last and route[2] in swapped)]

    def whole_copy(c, route):
        _, held, to, target = route
        return pltpu.make_async_remote_copy(
            src_ref=kv[held][c], dst_ref=kv[to][c], send_sem=seq_send.at[c, slot_of[id(route)]],
            recv_sem=seq_recv.at[c, where_of[to]], device_id=(target, me), device_id_type=MESH)

    def send(c, some):
        for route in used(c, some):
            @pl.when(route[0])
            def _(route=route):
                whole_copy(c, route).start()

    def send_part(c, which, group, src=None):
        for route in used(c, own_routes):
            @pl.when(route[0])
            def _(route=route):
                pltpu.make_async_remote_copy(
                    src_ref=rows_of(kv["own"][c], which, group) if src is None else src,
                    dst_ref=rows_of(kv[route[2]][c], which, group),
                    send_sem=seq_send.at[c, slot_of[id(route)]],
                    recv_sem=seq_recv.at[c, where_of[route[2]]],
                    device_id=(route[3], me), device_id_type=MESH).start()

    def both_of(buffer, group):
        if whole_blocks:
            return buffer.at[:, pl.ds(group * (rows // BLK), rows // BLK)]
        first = group * rows
        return buffer.at[:, first // BLK, pl.ds(pl.multiple_of(first % BLK, rows), rows), :]

    def send_both(c, group):
        for route in used(c, own_routes):
            @pl.when(route[0])
            def _(route=route):
                pltpu.make_async_remote_copy(
                    src_ref=both_of(kv["own"][c], group),
                    dst_ref=both_of(kv[route[2]][c], group),
                    send_sem=seq_send.at[c, slot_of[id(route)]],
                    recv_sem=seq_recv.at[c, where_of[route[2]]],
                    device_id=(route[3], me), device_id_type=MESH).start()

    def wait_for(c, name):
        @pl.when(there[name])
        def _():
            pltpu.make_async_remote_copy(
                src_ref=kv[name][c], dst_ref=kv[name][c], send_sem=seq_send.at[c, 0],
                recv_sem=seq_recv.at[c, where_of[name]], device_id=(sibling, me),
                device_id_type=MESH).wait_recv()

    def turn_keys(c):
        for r in range(1, groups):
            turn(k_ref, staged(stage_k, r, c, True), column_of((me + r) % groups, c), c, True)
        turn(k_ref, rows_of(kv["own"][c], 0, me), column_of(me, c), c, True)

    def enter_queries(c):
        for r in range(1, groups):
            turn(q_ref, staged(stage_q, r, c, False), column_of((me + r) % groups, c), c, False)
            in_copy(c, r, 2).start()
        turn(q_ref, q_all[c].at[my_rows, :], column_of(me, c), c, False)

    two = ("S", "XS", "ZXS")
    early_names = ("S", "XS", "X", "Zm", "Zp", "ZS")
    late_names = [n for n in names if n not in early_names + ("own", "ZXS")] + ["ZXS"]

    def paired(some):
        slots = [(name, j) for name in some for j in range(2 if name in two else 1)]
        return [slots[i:i + 2] for i in range(0, len(slots), 2)]

    own_groups = [[("own", 2 * i), ("own", 2 * i + 1)] for i in range(tokens // (2 * BLK))]
    early, late = paired(early_names), paired(late_names)

    def attend(c, units, begin, finish, first, count):
        @pl.loop(0, count)
        def _(i):
            b = first + i
            at = pl.ds(pl.multiple_of(b * BLK, BLK), BLK)
            table_row = frame * frame_blocks + b
            start = {}
            bound = {}
            for name, j in [slot for unit in units for slot in unit if slot[0] != "own"]:
                source = jnp.clip(place[name], 0, frames - 1)
                block = kv_ref[table_row, source * SLOTS + j] - source * frame_blocks
                start[name, j] = jnp.clip(block, 0, frame_blocks - 1)
                usable = jnp.where(there[name], count_ref[source, table_row], 0) > j
                bound[name, j] = jnp.where(usable, jnp.float32(jnp.inf), jnp.float32(-jnp.inf))
            for h in range(sizes[c]):
                col = slice(h * HD, (h + 1) * HD)
                query = q_all[c][at, col]
                kept = begins[c] // HD + h - kept_from

                def side(unit, which):
                    name, j = unit[0]
                    if name == "own":
                        return kv[name][c][which, j:j + 2, :, col].reshape(2 * BLK, HD)
                    parts = [kv[name][c][which, start[name, j], :, col] for name, j in unit]
                    return jnp.concatenate(parts, axis=0) if len(parts) > 1 else parts[0]

                top = None if begin else tops[kept, b]
                for u, unit in enumerate(units):
                    s = lax.dot_general(query, side(unit, 0), (((1,), (1,)), ((), ())),
                                        preferred_element_type=jnp.float32)
                    for k, slot in enumerate(unit):
                        part = s[:, k * BLK:(k + 1) * BLK]
                        if slot[0] != "own":
                            part = jnp.minimum(part, bound[slot])
                        scores[h, u, :, k * BLK:(k + 1) * BLK] = part
                        top = part if top is None else jnp.maximum(top, part)
                top = jnp.max(top, axis=1, keepdims=True)
                if begin:
                    total = None
                    out = None
                else:
                    factor = jnp.exp2((tops[kept, b] - top) * EXP2_SCALE)
                    total = sums[kept, b] * factor
                    out = numerators[kept, b] * factor
                for u, unit in enumerate(units):
                    p = jnp.exp2((scores[h, u, :, :len(unit) * BLK] - top) * EXP2_SCALE)
                    for k in range(len(unit)):
                        part = p[:, k * BLK:(k + 1) * BLK]
                        total = part if total is None else total + part
                    term = jnp.dot(p.astype(jnp.bfloat16), side(unit, 1), preferred_element_type=jnp.float32)
                    out = term if out is None else out + term
                if finish:
                    total = jnp.sum(total, axis=1, keepdims=True)
                    att[c][at, col] = (out / total).astype(jnp.bfloat16)
                else:
                    tops[kept, b] = jnp.broadcast_to(top, (BLK, BLK))
                    sums[kept, b] = total
                    numerators[kept, b] = out

    def fold(query, units, table_row):
        start, bound = {}, {}
        for u, unit in enumerate(units):
            for k, (buffer, source, exists, j) in enumerate(unit):
                if source is None:
                    continue
                clipped = jnp.clip(source, 0, frames - 1)
                block = kv_ref[table_row, clipped * SLOTS + j] - clipped * frame_blocks
                start[u, k] = jnp.clip(block, 0, frame_blocks - 1)
                usable = jnp.where(exists, count_ref[clipped, table_row], 0) > j
                bound[u, k] = jnp.where(usable, jnp.float32(jnp.inf), jnp.float32(-jnp.inf))

        def side(u, which):
            parts = [buffer[which, j if source is None else start[u, k]]
                     for k, (buffer, source, exists, j) in enumerate(units[u])]
            return jnp.concatenate(parts, axis=0) if len(parts) > 1 else parts[0]

        top = None
        for u, unit in enumerate(units):
            s = lax.dot_general(query, side(u, 0), (((1,), (1,)), ((), ())), preferred_element_type=jnp.float32)
            for k, slot in enumerate(unit):
                piece = s[:, k * BLK:(k + 1) * BLK]
                if slot[1] is not None:
                    piece = jnp.minimum(piece, bound[u, k])
                scores[0, u, :, k * BLK:(k + 1) * BLK] = piece
                top = piece if top is None else jnp.maximum(top, piece)
        top = jnp.maximum(jnp.max(top, axis=1, keepdims=True), -1e30)
        total, out = None, None
        for u, unit in enumerate(units):
            p = jnp.exp2((scores[0, u, :, :len(unit) * BLK] - top) * EXP2_SCALE)
            for k in range(len(unit)):
                piece = p[:, k * BLK:(k + 1) * BLK]
                total = piece if total is None else total + piece
            term = jnp.dot(p.astype(jnp.bfloat16), side(u, 1), preferred_element_type=jnp.float32)
            out = term if out is None else out + term
        return top, jnp.sum(total, axis=1, keepdims=True), out

    def diagonal():
        return (lax.broadcasted_iota(jnp.int32, (BLK, BLK), 0) == lax.broadcasted_iota(jnp.int32, (BLK, BLK), 1))

    share = max(rows // BLK, 1)

    def partial(name, queries, query_frame, units):
        @pl.loop(0, frame_blocks)
        def _(b):
            query = queries[pl.ds(pl.multiple_of(b * BLK, BLK), BLK), :]
            top, total, out = fold(query, units, query_frame * frame_blocks + b)
            inner = b % share
            half = b // share
            number = out / jnp.where(total > 0, total, 1.0)
            part[name][half, pl.ds(pl.multiple_of(inner * BLK, BLK), BLK), :] = number.astype(jnp.bfloat16)
            for k, column in enumerate((top, total)):
                flat = jnp.where(diagonal(), jnp.broadcast_to(column, (BLK, BLK)), 0.0)
                part_stat[name][half, pl.ds(4 * k + inner, 1), :] = jnp.sum(flat, axis=0, keepdims=True)

    def remote(src, dst, send, recv, seq, head):
        return pltpu.make_async_remote_copy(
            src_ref=src, dst_ref=dst, send_sem=swap_send.at[send], recv_sem=swap_recv.at[recv],
            device_id=(seq, head), device_id_type=MESH)

    middle = (frame >= 4) & (frame < 12)
    first_half = frame < 8
    over = frame + jnp.where(first_half, 4, -4)
    peer = (me + 1) % groups
    exists_of = {"E": always, "X": always, "8m": middle, "8p": middle}

    def queries_out(what):
        if what == 0:
            return always, remote(q_all[last], q_x, 0, 0, partner, me)
        if what == 1:
            return first_half, remote(q_all[last], q_8m, 1, 1, over, me)
        return jnp.logical_not(first_half), remote(q_all[last], q_8p, 2, 2, over, me)

    def sibling_keys():
        return remote(z_mine, z_theirs, 3, 3, sibling, me)

    def mine(source):
        return pltpu.make_async_copy(source, z_mine, swap_send.at[4])

    def across(i, stat):
        name = RESULTS[i]
        if stat:
            return remote(part_stat[name].at[peer], other_stat[name], 9 + i, 9 + i, frame, peer)
        return remote(part[name].at[peer], other[name], 5 + i, 5 + i, frame, peer)

    def returns(name):
        to, to_stat = (from_x, from_x_stat) if name == "X" else (from_8, from_8_stat)
        send = {"X": 13, "8m": 15, "8p": 17}[name]
        recv = 13 if name == "X" else 15
        target = {"X": partner, "8m": frame - 4, "8p": frame + 4}[name]
        return [
            remote(part_stat[name].at[me], to_stat.at[me], send + 1, recv + 1, target, me),
            remote(other_stat[name], to_stat.at[peer], send + 1, recv + 1, target, me),
            remote(part[name].at[me], to.at[me], send, recv, target, me),
            remote(other[name], to.at[peer], send, recv, target, me),
        ]

    def returned(name, to, to_stat):
        send = {"X": 13, "8m": 15, "8p": 17}[name]
        recv = 13 if name == "X" else 15
        return [remote(to, to, send, recv, partner, me), remote(to_stat, to_stat, send + 1, recv + 1, partner, me)]

    def swap_queries():
        for r in range(1, groups):
            in_wait(last, r, 2)
        for what in range(3):
            condition, copy = queries_out(what)

            @pl.when(condition)
            def _(copy=copy):
                copy.start()

    def swap_keys():
        for source, condition in (("Zm", high), ("Zp", low)):
            @pl.when(condition)
            def _(source=source):
                mine(kv[source][last]).start()
                mine(kv[source][last]).wait()
        sibling_keys().start()

    def swap_partials():
        own, beside, minus, plus = (kv[name][last] for name in ("own", "S", "Zm", "Zp"))
        for name in ("S", "ZS"):
            wait_for(last, name)

        @pl.when(middle)
        def _():
            remote(q_8m, q_8m, 1, 1, sibling, me).wait_recv()
            partial("8m", q_8m, frame - 4, [[(plus, frame + 4, middle, 0)]])
            remote(q_8p, q_8p, 2, 2, sibling, me).wait_recv()
            partial("8p", q_8p, frame + 4, [[(minus, frame - 4, middle, 0)]])
            for i in (2, 3):
                across(i, False).start()
                across(i, True).start()

        remote(q_x, q_x, 0, 0, sibling, me).wait_recv()
        sibling_keys().wait_recv()
        far = frame - side_pair
        far_there = (far >= 0) & (far < frames)
        sibling_far = sibling - side_pair
        partial("X", q_x, partner, [
            [(beside, sibling, always, 0), (beside, sibling, always, 1)],
            [(own, frame, always, 0), (z_mine, far, far_there, 0)],
            [(z_theirs, sibling_far, far_there, 0), (z_theirs, sibling_far, far_there, 1)],
        ])
        across(1, False).start()
        across(1, True).start()
        partial("E", q_all[last], frame, [
            [(own, None, None, 2 * i + k) for k in range(2)] for i in range(frame_blocks // 2)
        ] + [
            [(beside, sibling, always, 0), (beside, sibling, always, 1)],
            [(minus, place["Zm"], there["Zm"], 0), (plus, place["Zp"], there["Zp"], 0)],
            [(kv["ZS"][last], place["ZS"], there["ZS"], 0)],
        ])
        across(0, False).start()
        across(0, True).start()

    def swap_returns():
        for i in (2, 3, 1):
            name = RESULTS[i]

            @pl.when(exists_of[name])
            def _(i=i, name=name):
                across(i, False).wait_recv()
                across(i, True).wait_recv()
                for copy in returns(name):
                    copy.start()

    def column_from(flat):
        return jnp.sum(jnp.where(diagonal(), jnp.broadcast_to(flat, (BLK, BLK)), 0.0), axis=1, keepdims=True)

    def joined(stat_a, stat_b, i):
        top_a, top_b = stat_a[i:i + 1], stat_b[i:i + 1]
        top = jnp.maximum(top_a, top_b)
        weight_a = stat_a[4 + i:5 + i] * jnp.exp2((top_a - top) * EXP2_SCALE)
        weight_b = stat_b[4 + i:5 + i] * jnp.exp2((top_b - top) * EXP2_SCALE)
        total = weight_a + weight_b
        return top, total, weight_b / total

    def swap_near():
        across(0, False).wait_recv()
        across(0, True).wait_recv()
        for copy in returned("X", from_x, from_x_stat):
            copy.wait_recv()
        for g, group in enumerate((me, peer)):
            early_part, early_stat = (part["E"], part_stat["E"][me]) if g == 0 else (other["E"], other_stat["E"][...])
            x_stat = from_x_stat[group]
            for i in range(share):
                at = slice(i * BLK, (i + 1) * BLK)
                top, total, weight = joined(early_stat, x_stat, i)
                near_stat[g, i:i + 1, :] = top
                near_stat[g, 4 + i:5 + i, :] = total
                number = (early_part[me, at, :] if g == 0 else early_part[at, :]).astype(jnp.float32)
                near[g, at, :] = number + column_from(weight) * (from_x[group, at, :].astype(jnp.float32) - number)

    def swap_merge():
        for copy in returned("8m", from_8, from_8_stat):
            copy.wait_recv()
        for g, group in enumerate((me, peer)):
            col = pl.ds(column_of(group, last), HD)
            stat, stat_8 = near_stat[g], from_8_stat[group]
            for i in range(share):
                at = slice(i * BLK, (i + 1) * BLK)
                _, _, weight = joined(stat, stat_8, i)
                number = near[g, at, :]
                number = number + column_from(weight) * (from_8[group, at, :].astype(jnp.float32) - number)
                out_hbm[at, col] = number.astype(jnp.bfloat16)

    def swap_drain():
        for what in range(3):
            condition, copy = queries_out(what)

            @pl.when(condition)
            def _(copy=copy):
                copy.wait_send()
        sibling_keys().wait_send()
        for i, name in enumerate(RESULTS):
            @pl.when(exists_of[name])
            def _(i=i, name=name):
                across(i, False).wait_send()
                across(i, True).wait_send()
                if name != "E":
                    for copy in returned(name, from_x if name == "X" else from_8, from_x_stat if name == "X" else from_8_stat):
                        copy.wait_send()

    def out_copy(c, r):
        target = (me + r) % groups
        at = pl.ds(pl.multiple_of(target * rows, rows), rows)
        return pltpu.make_async_remote_copy(
            src_ref=att[c].at[at, :], dst_ref=out_hbm.at[:, pl.ds(column_of(me, c), widths[c])],
            send_sem=out_send.at[c, r - 1], recv_sem=out_recv.at[c, r - 1],
            device_id=(frame, target), device_id_type=MESH)

    def out_block(c, r, i):
        target = (me + r) % groups
        at = pl.ds(pl.multiple_of(target * rows + i * BLK, BLK), BLK)
        return pltpu.make_async_remote_copy(
            src_ref=att[c].at[at, :],
            dst_ref=out_hbm.at[pl.ds(i * BLK, BLK), pl.ds(column_of(me, c), widths[c])],
            send_sem=out_send.at[c, r - 1], recv_sem=out_recv.at[c, r - 1],
            device_id=(frame, target), device_id_type=MESH)

    def out_wait(c, r):
        source = (me + groups - r) % groups
        at = out_hbm.at[:, pl.ds(column_of(source, c), widths[c])]
        pltpu.make_async_remote_copy(
            src_ref=at, dst_ref=at, send_sem=out_send.at[c, r - 1],
            recv_sem=out_recv.at[c, r - 1], device_id=(frame, source),
            device_id_type=MESH).wait_recv()

    def local_out(c):
        return pltpu.make_async_copy(
            att[c].at[my_rows, :], out_hbm.at[:, pl.ds(column_of(me, c), widths[c])], out_local.at[c])

    def leave(c):
        for r in range(1, groups):
            out_copy(c, r).start()
        local_out(c).start()

    def enter_values(c):
        send_part(c, 1, me, value_columns(me, c))
        for r in range(1, groups):
            in_copy(c, r, 1).start()

    def enter_keys(c):
        turn_keys(c)
        send_part(c, 0, me)
        for r in range(1, groups):
            in_copy(c, r, 0).start()

    pl.semaphore_wait(barrier, expected)
    ahead = min(2, chunks)
    for c in range(ahead):
        enter_values(c)
    load_turn.wait()
    load_k.wait()
    for c in range(chunks):
        enter_keys(c)
        if c + ahead < chunks:
            enter_values(c + ahead)
    for c in range(chunks):
        local_value(c).start()
    load_q.start()
    load_kv.start()
    load_count.start()
    load_q.wait()
    load_kv.wait()
    load_count.wait()
    for c in ([last] if swap else []) + list(range(ends)):
        enter_queries(c)
    for name in names:
        if name in ("own", "S", "X", "XS"):
            continue

        @pl.when(jnp.logical_not(there[name]))
        def _(name=name):
            @pl.loop(0, frame_blocks)
            def _(i):
                for c in range(chunks):
                    for which in range(2):
                        kv[name][c][which, i] = jnp.zeros((BLK, widths[c]), jnp.bfloat16)

    for c in range(chunks):
        local_value(c).wait()
        for r in range(1, groups):
            for which in (1, 0):
                in_wait(c, r, which)
            send_both(c, (me + groups - r) % groups)
    if swap:
        swap_queries()
    for c in range(chunks):
        wait_for(c, "Zm")
        wait_for(c, "Zp")
        send(c, after_z)
        if c < ends:
            wait_for(c, "X")
            send(c, after_x)
        else:
            swap_keys()
    if swap:
        swap_partials()
    for c in range(one_pass, ends):
        for name in ("S", "XS", "ZS"):
            wait_for(c, name)
        for r in range(1, groups):
            in_wait(c, r, 2)
        attend(c, own_groups + early, True, False, 0, frame_blocks)

    if swap:
        swap_returns()

    def drain_out(c):
        for r in range(1, groups):
            out_copy(c, r).wait_send()
            out_wait(c, r)
        local_out(c).wait()

    for c in range(ends):
        wait_for(c, "ZX")
        send(c, after_zx)
        for power, some in after_power:
            wait_for(c, "M%d" % power)
            wait_for(c, "P%d" % power)
            send(c, some)
        if c == ends - 1:
            for d in range(chunks):
                for r in range(1, groups):
                    for what in range(3):
                        in_copy(d, r, what).wait_send()
            for route in routes:
                @pl.when(route[0])
                def _(route=route):
                    for d in range(ends - 1):
                        whole_copy(d, route).wait_send()
            for d in range(ends - 2):
                drain_out(d)
        if len(names) > 9:
            wait_for(c, names[-1])
        for name in ("S", "XS", "ZS", "ZXS") if c < one_pass else ("ZXS",):
            wait_for(c, name)
        for r in range(1, groups):
            if c < one_pass:
                in_wait(c, r, 2)
        if c < one_pass:
            attend(c, own_groups + early + late, True, True, 0, frame_blocks)
            leave(c)
        elif whole_blocks:
            share = rows // BLK
            for r in range(1, groups):
                for i in range(share):
                    attend(c, late, False, True, (me + r) % groups * share + i, 1)
                    out_block(c, r, i).start()
            attend(c, late, False, True, me * share, share)
            local_out(c).start()
        else:
            attend(c, late, False, True, 0, frame_blocks)
            leave(c)

    for route in routes:
        @pl.when(route[0])
        def _(route=route):
            for c in range(ends - 1, chunks):
                if used(c, [route]):
                    whole_copy(c, route).wait_send()
    for c in range(max(ends - 2, 0), ends):
        drain_out(c)
    if swap:
        swap_near()
        swap_drain()
        swap_merge()


def local(queries, keys, values, kv_blocks, block_counts):
    frames = lax.axis_size("seq")
    groups = lax.axis_size("head")
    rows, model = queries.shape
    heads = model // HD // groups
    sizes = chunk_sizes(heads)
    chunks = len(sizes)
    tokens = rows * groups
    names = source_names(frames)
    n_pairs = tokens // (2 * BLK) + (len(names) + 4) // 2
    plan = (frames, groups, rows, heads, sizes, tuple(names))
    n_routes = 10 + 2 * len(names)
    lead = (rows // BLK, BLK) if rows % BLK == 0 else (rows,)
    blocks = [pltpu.VMEM((2, tokens // BLK, BLK, size * HD), jnp.bfloat16) for size in sizes]
    flats = [pltpu.VMEM((tokens, size * HD), jnp.bfloat16) for size in sizes]
    group_width = heads * HD
    whole = pltpu.VMEM((rows, model), jnp.bfloat16)
    stage_q = pltpu.VMEM((max(groups - 1, 1), rows, group_width), jnp.bfloat16)
    stage_k = pltpu.VMEM((max(groups - 1, 1),) + lead + (group_width,), jnp.bfloat16)
    state = pltpu.VMEM((sum(sizes[-TWO_PASS:]), tokens // BLK, BLK, HD), jnp.float32)
    sem = pltpu.SemaphoreType.DMA
    others = max(groups - 1, 1)
    swap_scratch = []
    if swaps(frames, groups, rows, sizes):
        half = pltpu.VMEM((rows, HD), jnp.bfloat16)
        halves = pltpu.VMEM((groups, rows, HD), jnp.bfloat16)
        stat = pltpu.VMEM((8, BLK), jnp.float32)
        stats = pltpu.VMEM((groups, 8, BLK), jnp.float32)
        swap_scratch = [pltpu.VMEM((tokens, HD), jnp.bfloat16)] * 3 + [blocks[-1]] * 2 + [halves, halves, stats, stats]
        swap_scratch += [halves] * 4 + [stats] * 4 + [half] * 4 + [stat] * 4
        swap_scratch += [pltpu.VMEM((groups, rows, HD), jnp.float32), stats, sem((20,)), sem((20,))]
    return pl.pallas_call(
        functools.partial(kernel, plan),
        out_shape=jax.ShapeDtypeStruct((rows, model), jnp.bfloat16),
        in_specs=[
            pl.BlockSpec(memory_space=pltpu.HBM),
            pl.BlockSpec(memory_space=pltpu.HBM),
            pl.BlockSpec(memory_space=pltpu.HBM),
            pl.BlockSpec(memory_space=pltpu.HBM),
            pl.BlockSpec(memory_space=pltpu.HBM),
            pl.BlockSpec(memory_space=pltpu.HBM),
        ],
        out_specs=pl.BlockSpec(memory_space=pltpu.VMEM),
        scratch_shapes=blocks * len(names) + flats * 2 + [
            pltpu.SMEM(kv_blocks.shape, jnp.int32),
            pltpu.SMEM(block_counts.shape[::-1], jnp.int32),
            pltpu.VMEM((8, HD), jnp.float32),
            whole,
            whole,
            stage_k,
            stage_q,
            pltpu.VMEM((max(sizes), n_pairs, BLK, 2 * BLK), jnp.float32),
            state,
            state,
            state,
            sem((chunks, others, 3)),
            sem((chunks, others, 3)),
            sem((chunks,)),
            sem((chunks, n_routes)),
            sem((chunks, len(names))),
            sem((chunks, others)),
            sem((chunks, others)),
            sem((chunks,)),
            sem((5,)),
        ] + swap_scratch,
        compiler_params=pltpu.CompilerParams(
            collective_id=0, has_side_effects=True, vmem_limit_bytes=50 * 1024 * 1024
        ),
    )(*[pltpu.with_memory_space_constraint(x, pltpu.HBM) for x in (
        kv_blocks, block_counts.T, jnp.asarray(turn_table(frames)), queries, keys,
        values.reshape(lead + (model,)))])


def solution(mesh):
    in_specs = (
        P(("seq", "head"), None),
        P(("seq", "head"), None),
        P(("seq", "head"), None),
        P(),
        P(),
    )
    out_specs = P(("seq", "head"), None)
    return jax.shard_map(local, mesh=mesh, in_specs=in_specs, out_specs=out_specs, check_vma=False)
```
